128 devices in a mesh: lat: 4 (over x_hi, core), lon: 32 (over z, x_lo, y).
Axes of the slice: x: 4 (x_hi: 2, x_lo: 2; x = x_hi * 2 + x_lo), y: 4, z: 4, core: 2. Of those that a mesh axis runs over, the one named last changes fastest.
Arguments:
- tokens: bfloat16 [4, 48, 384, 512], P(None, 'lat', 'lon'), may hold values from -6 to 6
- region: int32 [4, 48, 384], P(None, 'lat', 'lon'), may hold values from 0 to 2
- norm_gain1: float32 [2, 512], replicated, may hold values from 0.25 to 1.75
- qkv_weight: bfloat16 [2, 512, 1536], replicated, may hold values from -3 to 3
- proj_weight: bfloat16 [2, 512, 512], replicated, may hold values from -0.25 to 0.25
- norm_gain2: float32 [2, 512], replicated, may hold values from 0.25 to 1.75
- up_weight: bfloat16 [2, 512, 2048], replicated, may hold values from -0.25 to 0.25
- down_weight: bfloat16 [2, 2048, 512], replicated, may hold values from -0.125 to 0.125
Outputs:
- result: bfloat16 [4, 48, 384, 512], P(None, 'lat', 'lon')
The draws below stay inside these ranges and needn't reach their ends.
All inputs are finite; a program needn't handle non-finite values.
Results may differ from the reference program's by a relative error of at most 0.012.
Values may be sent and summed in bfloat16 or wider, within the bound.
No kernel may reach another device: no remote copies, remote signals or barrier semaphores. Data moves between devices by JAX's collectives and lax.ppermute only.
A program may use at most 64 MiB of HBM per device.

```python
import math
import jax
import jax.numpy as jnp
from jax import lax

D = 512
FF = 2048
HEADS = 8
LEV = 4
WLEV = 2
WLAT = 6
WLON = 12
NLAT = 48
NLON = 384


def draw_qkv_weight(key, part):
    first_key = jax.random.fold_in(jax.random.fold_in(key, 17), 0)
    base = jax.random.normal(first_key, (2, D, 3 * D), jnp.float32) / math.sqrt(D)
    return base.astype(jnp.bfloat16)


def plant(values, key, least, largest):
    longest = values.shape.index(max(values.shape))
    spots = []
    for shift in (0, 1):
        where = [jax.random.randint(jax.random.fold_in(key, axis), (), 0, length) for axis, length in enumerate(values.shape)]
        where[longest] = (where[longest] + shift) % values.shape[longest]
        spots.append(tuple(where))
    return values.at[spots[0]].set(least).at[spots[1]].set(largest)


def block_levels(rng, shape, cuts, low, largest):
    factor_of, own = 1.0, jax.random.fold_in(rng, 6)
    for axis_at, parts in cuts:
        steps = jnp.exp(jax.random.uniform(jax.random.fold_in(own, axis_at), (parts,), jnp.float32, low / len(cuts), largest / len(cuts)))
        factor_of = factor_of * jnp.repeat(steps, shape[axis_at] // parts).reshape([-1 if axis == axis_at else 1 for axis in range(len(shape))])
    return factor_of


def bell_draw(key, extent, scale, limit, cuts=(), held_as=jnp.bfloat16):
    drawn = jax.random.normal(key, extent, jnp.float32) * scale
    if len(cuts) > 0:
        drawn = block_levels(key, extent, cuts, -0.22, 0.18) * drawn
    return jnp.clip(drawn, min=-limit, max=limit).astype(held_as)


def setup_inputs(seed: int = 0) -> dict:
    splits = jax.random.split(jax.random.key(seed), 9)
    tokens = bell_draw(splits[0], (LEV, NLAT, NLON, D), 1.0, 6.0, ((1, 4), (2, 32)))
    region = plant(jax.random.randint(splits[1], (LEV, NLAT, NLON), 0, 3), jax.random.fold_in(splits[1], 1), 0, 2).astype(jnp.int32)
    norm_gain1 = jnp.clip(1.0 + 0.15 * jax.random.normal(splits[2], (2, D), jnp.float32), 0.25, 1.75)
    qkv_weight = draw_qkv_weight(jax.random.fold_in(splits[8], 71), 0)
    proj_weight = bell_draw(splits[4], (2, D, D), D ** -0.5, 0.25)
    norm_gain2 = jnp.clip(1.0 + 0.15 * jax.random.normal(splits[5], (2, D), jnp.float32), 0.25, 1.75)
    up_weight = bell_draw(splits[6], (2, D, FF), D ** -0.5, 0.25)
    down_weight = bell_draw(splits[7], (2, FF, D), FF ** -0.5, 0.125)
    return {"tokens": tokens, "region": region, "norm_gain1": norm_gain1, "qkv_weight": qkv_weight, "proj_weight": proj_weight, "norm_gain2": norm_gain2, "up_weight": up_weight, "down_weight": down_weight}


epsilon = 1e-05

def layer_norm(field, gain_vector):
    field = field.astype(jnp.float32)
    average = lax.optimization_barrier(jnp.mean(field, axis=-1, keepdims=True))
    centered = field - average
    variance = lax.optimization_barrier(jnp.mean(centered * centered, axis=-1, keepdims=True))
    return centered * lax.rsqrt(variance + epsilon) * gain_vector

def to_windows(field):
    level_count, row_count, column_count = field.shape[:3]
    trailing = tuple(field.shape[3:])
    shaped = field.reshape((level_count // WLEV, WLEV, row_count // WLAT, WLAT, column_count // WLON, WLON) + trailing)
    order = (0, 2, 4, 1, 3, 5) + tuple(range(6, 6 + len(trailing)))
    return jnp.transpose(shaped, order).reshape((-1, WLEV * WLAT * WLON) + trailing)

def from_windows(windows, level_count, row_count, column_count):
    trailing = tuple(windows.shape[2:])
    shaped = windows.reshape((level_count // WLEV, row_count // WLAT, column_count // WLON, WLEV, WLAT, WLON) + trailing)
    order = (0, 3, 1, 4, 2, 5) + tuple(range(6, 6 + len(trailing)))
    return jnp.transpose(shaped, order).reshape((level_count, row_count, column_count) + trailing)

def window_attention(normed, labels, w_qkv, w_proj):
    count, span, features = normed.shape
    head_size = features // HEADS
    mixed = jnp.dot(normed, w_qkv, preferred_element_type=jnp.float32).astype(jnp.bfloat16)
    queries = mixed[..., :features].reshape(count, span, HEADS, head_size).astype(jnp.float32)
    key_vectors = mixed[..., features:2 * features].reshape(count, span, HEADS, head_size).astype(jnp.float32)
    values = mixed[..., 2 * features:].reshape(count, span, HEADS, head_size).astype(jnp.float32)
    scores = jnp.einsum('wqhd,wkhd->whqk', queries, key_vectors) * (1.0 / math.sqrt(head_size))
    allowed = labels[:, None, :, None] == labels[:, None, None, :]
    scores = jnp.where(allowed, scores, -jnp.inf)
    peak = lax.optimization_barrier(jnp.max(scores, axis=-1, keepdims=True))
    exponent = jnp.exp(scores - peak)
    attention_weights = (exponent / lax.optimization_barrier(jnp.sum(exponent, axis=-1, keepdims=True))).astype(jnp.bfloat16)
    gathered = jnp.einsum('whqk,wkhd->wqhd', attention_weights.astype(jnp.float32), values)
    gathered = gathered.astype(jnp.bfloat16).reshape(count, span, features)
    return jnp.dot(gathered, w_proj, preferred_element_type=jnp.float32)

def attention_part(field, labels, gain_vector, w_qkv, w_proj):
    level_count, row_count, column_count, features = field.shape
    normed = layer_norm(field, gain_vector).astype(jnp.bfloat16)
    windows = to_windows(normed)
    window_labels = to_windows(labels)
    per_row = column_count // WLON
    groups = windows.reshape((-1, per_row) + tuple(windows.shape[1:]))
    label_groups = window_labels.reshape((-1, per_row) + tuple(window_labels.shape[1:]))

    def attend(pair):
        return window_attention(pair[0], pair[1], w_qkv, w_proj)
    projected = lax.map(attend, (groups, label_groups)).reshape(windows.shape)
    return field.astype(jnp.float32) + from_windows(projected, level_count, row_count, column_count)

def feed_forward(field, gain_vector, w_up, w_down):

    def per_level(level_field):
        normed = layer_norm(level_field, gain_vector).astype(jnp.bfloat16)
        hidden_units = jax.nn.gelu(jnp.dot(normed, w_up, preferred_element_type=jnp.float32)).astype(jnp.bfloat16)
        return (level_field + jnp.dot(hidden_units, w_down, preferred_element_type=jnp.float32)).astype(jnp.bfloat16)
    return lax.map(per_level, field)

def reference(tokens, region, norm_gain1, qkv_weight, proj_weight, norm_gain2, up_weight, down_weight):
    half_level = WLEV // 2
    half_row = WLAT // 2
    half_column = WLON // 2
    mixed_first = attention_part(tokens, region, norm_gain1[0], qkv_weight[0], proj_weight[0])
    first_out = feed_forward(mixed_first, norm_gain2[0], up_weight[0], down_weight[0])
    rolled = jnp.roll(first_out, (-half_level, -half_row, -half_column), (0, 1, 2))
    rolled_region = jnp.roll(region, (-half_level, -half_row, -half_column), (0, 1, 2))
    level_index = jnp.arange(LEV, dtype=jnp.int32)[:, None, None]
    row_index = jnp.arange(NLAT, dtype=jnp.int32)[None, :, None]
    wrapped_level = (level_index >= LEV - half_level).astype(jnp.int32)
    wrapped_row = (row_index >= NLAT - half_row).astype(jnp.int32)
    labels_second = rolled_region * 4 + wrapped_level * 2 + wrapped_row
    mixed_second = attention_part(rolled, labels_second, norm_gain1[1], qkv_weight[1], proj_weight[1])
    restored = jnp.roll(mixed_second, (half_level, half_row, half_column), (0, 1, 2))
    return feed_forward(restored, norm_gain2[1], up_weight[1], down_weight[1])
```

```python
import math

import jax
import jax.numpy as jnp
import numpy as np
from jax import lax
from jax.experimental import pallas as pl
from jax.experimental.pallas import tpu as pltpu
from jax.sharding import PartitionSpec as P

BF = jnp.bfloat16
F32 = jnp.float32
LEV, D, FF, HEADS, HD = 4, 512, 2048, 8, 64
ROWS = COLS = 12
UNIT = 18
GROUP = LEV * UNIT
PER_RT = 2 * GROUP
NPAD = LEV * 3 * 16
EPS = 1e-05
BIG = 1e30
EXP_SCALE = math.log2(math.e) / math.sqrt(HD)
VMEM_LIMIT = 56 * 1024 * 1024
FCHUNK = 512


def permutation():
    p = np.zeros((PER_RT, NPAD), np.float32)
    for half in range(2):
        for level in range(LEV):
            for row in range(3):
                for col in range(6):
                    to = half * GROUP + level * UNIT + row * 6 + col
                    p[to, (level * 3 + row) * 16 + half * 6 + col] = 1.0
    return p


def layer_norm(x, gain):
    mean = jnp.mean(x, axis=-1, keepdims=True)
    centered = x - mean
    variance = jnp.mean(centered * centered, axis=-1, keepdims=True)
    return centered * lax.rsqrt(variance + EPS) * gain


def one_hot(labels, rows):
    lane = lax.broadcasted_iota(jnp.int32, (rows, 128), 1) & 63
    return lane.astype(F32) == labels


def query_features(labels, rows):
    return jnp.where(one_hot(labels, rows), -BIG, 0.0).astype(BF)


def key_features(labels, rows):
    return jnp.where(one_hot(labels, rows), 0.0, 1.0).astype(BF)


def low_lanes(rows):
    return lax.broadcasted_iota(jnp.int32, (rows, 128), 1) < 64


def attend(q, k, v, qf, kf):
    m, n = q.shape[0], k.shape[0]
    low_q, low_k = low_lanes(m), low_lanes(n)
    ones = jnp.ones((n, 128), BF)
    tiles = []
    for pair in range(HEADS // 2):
        lanes = slice(pair * 128, (pair + 1) * 128)
        qt, kt, vt = q[:, lanes], k[:, lanes], v[:, lanes]
        got = []
        for odd in range(2):
            if odd:
                qh, kh, vh = jnp.where(low_q, qf, qt), jnp.where(low_k, kf, kt), jnp.where(low_k, ones, vt)
            else:
                qh, kh, vh = jnp.where(low_q, qt, qf), jnp.where(low_k, kt, kf), jnp.where(low_k, vt, ones)
            s = lax.dot_general(qh, kh, (((1,), (1,)), ((), ())), preferred_element_type=F32)
            peak = jnp.max(s, axis=-1, keepdims=True)
            e = jnp.exp2((s - peak) * EXP_SCALE).astype(BF)
            got.append(jnp.dot(e, vh, preferred_element_type=F32))
        num = jnp.where(low_q, got[0], got[1])
        den = pltpu.roll(jnp.where(low_q, got[1], got[0]), 64, 1)
        tiles.append(num / den)
    return jnp.concatenate(tiles, axis=1)


def mlp(h, gain, wup, wdown):
    a = layer_norm(h, gain).astype(BF)
    acc = h
    for c in range(0, FF, FCHUNK):
        u = jnp.dot(a, wup[:, c : c + FCHUNK], preferred_element_type=F32)
        g = jax.nn.gelu(u).astype(BF)
        acc = acc + jnp.dot(g, wdown[c : c + FCHUNK, :], preferred_element_type=F32)
    return acc


class Weights:
    def __init__(self, block, sources, buffers, sem):
        self.copies = [
            pltpu.make_async_copy(s.at[block], b, sem.at[i]) for i, (s, b) in enumerate(zip(sources, buffers))
        ]
        for c in self.copies:
            c.start()

    def wait(self, i):
        self.copies[i].wait()


WEIGHT_SCRATCH = [
    pltpu.VMEM((D, 3 * D), BF),
    pltpu.VMEM((D, D), BF),
    pltpu.VMEM((D, FF), BF),
    pltpu.VMEM((FF, D), BF),
    pltpu.SemaphoreType.DMA((4,)),
]


def first_kernel(
    x_ref, lab_ref, labrow_ref, p_ref, g1_ref, g2_ref, wq_hbm, wp_hbm, wu_hbm, wd_hbm,
    own_ref, up_ref, down_ref, left_ref, right_ref,
    xp, wq, wp, wu, wd, sem,
):
    weights = Weights(0, (wq_hbm, wp_hbm, wu_hbm, wd_hbm), (wq, wp, wu, wd), sem)
    xp[...] = jnp.zeros_like(xp)
    for rt in range(4):
        for level in range(LEV):
            for row in range(3):
                xp[rt, level * 3 + row, 0:COLS, :] = x_ref[level, rt * 3 + row]
    g1, g2 = g1_ref[0:1, :], g2_ref[0:1, :]
    for half in range(2):
        x = jnp.concatenate(
            [
                jnp.dot(p_ref[...], xp[rt].reshape(NPAD, D), preferred_element_type=F32)
                for rt in (2 * half, 2 * half + 1)
            ],
            axis=0,
        )
        a = layer_norm(x, g1).astype(BF)
        if half == 0:
            weights.wait(0)
        qkv = jnp.dot(a, wq[...], preferred_element_type=F32).astype(BF)
        lab = lab_ref[half * 288 : half * 288 + 288, 0:1]
        o = attend(
            qkv[:, :D], qkv[:, D : 2 * D], qkv[:, 2 * D :], query_features(lab, 288), key_features(lab, 288)
        ).astype(BF)
        if half == 0:
            weights.wait(1)
        h = x + jnp.dot(o, wp[...], preferred_element_type=F32)
        if half == 0:
            weights.wait(2)
            weights.wait(3)
        y = mlp(h, g2, wu, wd)
        for i in range(2):
            rt = 2 * half + i
            for side in range(2):
                part = y[(2 * i + side) * GROUP : (2 * i + side + 1) * GROUP].astype(BF)
                own_ref[rt * 2 + side] = part
                (left_ref, right_ref)[side][rt * GROUP : (rt + 1) * GROUP, :] = part
                if rt == 0:
                    up_ref[side * GROUP : (side + 1) * GROUP, :] = part
                if rt == 3:
                    down_ref[side * GROUP : (side + 1) * GROUP, :] = part
    up_ref[PER_RT:, :] = labrow_ref[0]
    down_ref[PER_RT:, :] = labrow_ref[1]
    left_ref[4 * GROUP :, :] = labrow_ref[2]
    right_ref[4 * GROUP :, :] = labrow_ref[3]


def column_of(rows, count):
    return jnp.transpose(rows.astype(F32)[:, :count], (1, 0))[:, 0:1]


def second_body(windows, labels_of, p_ref, g1_ref, g2_ref, hbm, out_hbm, scratch, rts):
    wq, wp, wu, wd, sem, o_s, x_s, y_s, out_sem = scratch
    weights = Weights(1, hbm, (wq, wp, wu, wd), sem)
    g1, g2 = g1_ref[1:2, :], g2_ref[1:2, :]
    for index, (own, halo) in enumerate(windows):
        n_own = len(own) * GROUP
        x = jnp.concatenate([s[0].astype(F32) for s in own + halo], axis=0)
        lab = jnp.concatenate([s[1] for s in own + halo], axis=0)
        a = layer_norm(x, g1).astype(BF)
        if index == 0:
            weights.wait(0)
        kv = jnp.dot(a, wq[:, D:], preferred_element_type=F32).astype(BF)
        q = jnp.dot(a[:n_own], wq[:, :D], preferred_element_type=F32).astype(BF)
        o = attend(q, kv[:, :D], kv[:, D:], query_features(lab[:n_own], n_own), key_features(lab, 288))
        for i, s in enumerate(own):
            rows = slice(s[2] * GROUP, (s[2] + 1) * GROUP)
            o_s[rows, :] = o[i * GROUP : (i + 1) * GROUP]
            x_s[rows, :] = x[i * GROUP : (i + 1) * GROUP]
    weights.wait(1)
    h = x_s[...] + jnp.dot(o_s[...].astype(BF), wp[...], preferred_element_type=F32)
    weights.wait(2)
    weights.wait(3)
    y = mlp(h, g2, wu, wd).astype(BF)
    copies = []
    for i, rt in enumerate(rts):
        nat = lax.dot_general(
            p_ref[...], y[i * PER_RT : (i + 1) * PER_RT], (((0,), (0,)), ((), ())), preferred_element_type=F32
        ).astype(BF).reshape(LEV * 3, 16, D)
        for level in range(LEV):
            for row in range(3):
                y_s[i, level, row] = nat[level * 3 + row, :COLS]
        c = pltpu.make_async_copy(y_s.at[i], out_hbm.at[:, rt * 3 : rt * 3 + 3], out_sem.at[i])
        c.start()
        copies.append(c)
    for c in copies:
        c.wait()


def middle_kernel(
    own_ref, lh_ref, rh_ref, lab_ref, p_ref, g1_ref, g2_ref, wq_hbm, wp_hbm, wu_hbm, wd_hbm, out_hbm, *scratch
):
    windows = []
    for side, halo_ref in enumerate((lh_ref, rh_ref)):
        col = column_of(halo_ref[4 * GROUP :, :], 384)
        own = [
            (own_ref[rt * 2 + side], lab_ref[(rt * 2 + side) * GROUP : (rt * 2 + side + 1) * GROUP, 1:2], (rt - 1) * 2 + side)
            for rt in (1, 2)
        ]
        halo = [
            (halo_ref[rt * GROUP : (rt + 1) * GROUP, :], col[rt * GROUP : (rt + 1) * GROUP]) for rt in (1, 2)
        ]
        windows.append((own, halo))
    second_body(windows, None, p_ref, g1_ref, g2_ref, (wq_hbm, wp_hbm, wu_hbm, wd_hbm), out_hbm, scratch, (1, 2))


def edge_kernel(
    out_in, own_ref, u_ref, d_ref, lh_ref, rh_ref, lhh_ref, rhh_ref, lab_ref, p_ref, g1_ref, g2_ref,
    wq_hbm, wp_hbm, wu_hbm, wd_hbm, out_hbm, *scratch
):
    windows = []
    for rt, v_ref in ((0, u_ref), (3, d_ref)):
        vcol = column_of(v_ref[PER_RT:, :], 256)
        at = 0 if rt == 0 else 1
        for side, (h_ref, hh_ref) in enumerate(((lh_ref, lhh_ref), (rh_ref, rhh_ref))):
            hcol = column_of(h_ref[4 * GROUP :, :], 384)
            other = 1 - side
            hvcol = column_of(hh_ref[PER_RT + 8 * at : PER_RT + 8 * at + 8, :], 256)
            own = [
                (own_ref[rt * 2 + side], lab_ref[(rt * 2 + side) * GROUP : (rt * 2 + side + 1) * GROUP, 1:2], at * 2 + side)
            ]
            halo = [
                (v_ref[side * GROUP : (side + 1) * GROUP, :], vcol[side * GROUP : (side + 1) * GROUP]),
                (h_ref[rt * GROUP : (rt + 1) * GROUP, :], hcol[rt * GROUP : (rt + 1) * GROUP]),
                (hh_ref[at * GROUP : (at + 1) * GROUP, :], hvcol[other * GROUP : (other + 1) * GROUP]),
            ]
            windows.append((own, halo))
    second_body(windows, None, p_ref, g1_ref, g2_ref, (wq_hbm, wp_hbm, wu_hbm, wd_hbm), out_hbm, scratch, (0, 3))


SECOND_SCRATCH = WEIGHT_SCRATCH + [
    pltpu.VMEM((4 * GROUP, D), F32),
    pltpu.VMEM((4 * GROUP, D), F32),
    pltpu.VMEM((2, LEV, 3, COLS, D), BF),
    pltpu.SemaphoreType.DMA((2,)),
]

VM = pl.BlockSpec(memory_space=pltpu.VMEM)
ANY = pl.BlockSpec(memory_space=pl.ANY)


def cost(flops, nbytes):
    return pl.CostEstimate(flops=int(flops), bytes_accessed=int(nbytes), transcendentals=0)


def shift(value, axis, steps):
    count = lax.axis_size(axis)
    return lax.ppermute(value, axis, [(s, (s + steps) % count) for s in range(count)])


def per_device(tokens, region, norm_gain1, qkv_weight, proj_weight, norm_gain2, up_weight, down_weight):
    p = jnp.asarray(permutation(), BF)
    tr = region.reshape(LEV, 4, 3, 2, 6).transpose(1, 3, 0, 2, 4)
    level = jnp.arange(LEV, dtype=jnp.int32)[None, None, :, None, None]
    row = (
        lax.axis_index("lat") * ROWS
        + 3 * jnp.arange(4, dtype=jnp.int32)[:, None, None, None, None]
        + jnp.arange(3, dtype=jnp.int32)[None, None, None, :, None]
    )
    lab1 = (tr * 2 + level // 2).reshape(576)
    pair = jnp.where((level == 1) | (level == 2), 0, 1)
    lab2 = ((tr * 4 + 2 * (level == 0) + (row < 3)) * 2 + pair).reshape(4, 2, GROUP)
    labs = jnp.stack([lab1, lab2.reshape(576)], axis=1).astype(F32)

    def as_row(v):
        return jnp.pad(v.reshape(-1), (0, 512 - v.size))

    rows = jnp.stack([as_row(lab2[0]), as_row(lab2[3]), as_row(lab2[:, 0]), as_row(lab2[:, 1])])
    labrow = jnp.broadcast_to(rows[:, None, :], (4, 8, 512)).astype(BF)

    weights = (qkv_weight, proj_weight, up_weight, down_weight)
    params = pltpu.CompilerParams(vmem_limit_bytes=VMEM_LIMIT)
    own, up, down, left, right = pl.pallas_call(
        first_kernel,
        out_shape=(
            jax.ShapeDtypeStruct((8, GROUP, D), BF),
            jax.ShapeDtypeStruct((PER_RT + 8, D), BF),
            jax.ShapeDtypeStruct((PER_RT + 8, D), BF),
            jax.ShapeDtypeStruct((4 * GROUP + 8, D), BF),
            jax.ShapeDtypeStruct((4 * GROUP + 8, D), BF),
        ),
        in_specs=[VM] * 6 + [ANY] * 4,
        out_specs=[VM] * 5,
        scratch_shapes=[pltpu.VMEM((4, LEV * 3, 16, D), BF)] + WEIGHT_SCRATCH,
        compiler_params=params,
        cost_estimate=cost(4e9, 8e6),
        name="first_block",
    )(tokens, labs, labrow, p, norm_gain1, norm_gain2, *weights)

    below = shift(up, "lat", -1)
    above = shift(down, "lat", 1)
    right_halo = shift(left, "lon", -1)
    left_halo = shift(right, "lon", 1)
    to_left = jnp.concatenate([above[:GROUP], below[:GROUP], above[PER_RT:], below[PER_RT:]], axis=0)
    to_right = jnp.concatenate([above[GROUP:PER_RT], below[GROUP:PER_RT], above[PER_RT:], below[PER_RT:]], axis=0)
    right_corner = shift(to_left, "lon", -1)
    left_corner = shift(to_right, "lon", 1)

    out_shape = jax.ShapeDtypeStruct((LEV, ROWS, COLS, D), BF)
    out = pl.pallas_call(
        middle_kernel,
        out_shape=out_shape,
        in_specs=[VM] * 7 + [ANY] * 4,
        out_specs=ANY,
        scratch_shapes=SECOND_SCRATCH,
        compiler_params=params,
        cost_estimate=cost(2.5e9, 8e6),
        name="second_middle",
    )(own, left_halo, right_halo, labs, p, norm_gain1, norm_gain2, *weights)
    return pl.pallas_call(
        edge_kernel,
        out_shape=out_shape,
        in_specs=[ANY] + [VM] * 11 + [ANY] * 4,
        out_specs=ANY,
        scratch_shapes=SECOND_SCRATCH,
        input_output_aliases={0: 0},
        compiler_params=params,
        cost_estimate=cost(2.5e9, 8e6),
        name="second_edge",
    )(out, own, above, below, left_halo, right_halo, left_corner, right_corner, labs, p, norm_gain1, norm_gain2, *weights)


def solution(mesh):
    return jax.shard_map(
        per_device,
        mesh=mesh,
        in_specs=(P(None, "lat", "lon", None), P(None, "lat", "lon"), P(), P(), P(), P(), P(), P()),
        out_specs=P(None, "lat", "lon", None),
        check_vma=False,
    )
```

```python
import math

import jax
import jax.numpy as jnp
import numpy as np
from jax import lax
from jax.experimental import pallas as pl
from jax.experimental.pallas import tpu as pltpu
from jax.sharding import PartitionSpec as P

BF = jnp.bfloat16
F32 = jnp.float32
LEV, D, FF, HEADS, HD = 4, 512, 2048, 8, 64
ROWS = COLS = 12
PIECE = 6 * LEV
GROUP = 3 * PIECE
PER_RT = 2 * GROUP
HALF = 2 * PER_RT
TOKENS = 2 * HALF
EPS = 1e-05
BIG = 1e30
EXP_SCALE = math.log2(math.e) / math.sqrt(HD)
VMEM_LIMIT = 56 * 1024 * 1024
FCHUNK = 512
STAGE = 8


def token_tables():
    pick = np.zeros((HALF, 128), np.float32)
    lane = np.zeros((HALF, 128), np.float32)
    for row in range(6):
        for col in range(COLS):
            for level in range(LEV):
                t = (row * COLS + col) * LEV + level
                pick[t, row * LEV + level] = 1.0
                lane[t, col] = 1.0
    level = np.arange(HALF) % LEV
    row = np.arange(HALF) // (COLS * LEV)
    adds = np.zeros((HALF, 128), np.float32)
    adds[:, 0] = level // 2
    adds[:, 1] = 4 * (level == 0) + np.where((level == 1) | (level == 2), 0, 1)
    adds[:, 2] = 2 * (row < 3)
    return pick, lane, adds


def layer_norm(x, gain):
    mean = jnp.mean(x, axis=-1, keepdims=True)
    centered = x - mean
    variance = jnp.mean(centered * centered, axis=-1, keepdims=True)
    return centered * lax.rsqrt(variance + EPS) * gain


def one_hot(labels, rows):
    lane = lax.broadcasted_iota(jnp.int32, (rows, 128), 1) & 63
    return lane.astype(F32) == labels


def query_features(labels, rows):
    return jnp.where(one_hot(labels, rows), -BIG, 0.0).astype(BF)


def key_features(labels, rows):
    return jnp.where(one_hot(labels, rows), 0.0, 1.0).astype(BF)


def low_lanes(rows):
    return lax.broadcasted_iota(jnp.int32, (rows, 128), 1) < 64


def attend(q, k, v, qf, kf):
    m, n = q.shape[0], k.shape[0]
    low_q, low_k = low_lanes(m), low_lanes(n)
    ones = jnp.ones((n, 128), BF)
    tiles = []
    for first in range(0, HEADS, STAGE):
        heads = range(first, first + STAGE)
        scores, weights, got = [], [], []
        for h in heads:
            lanes = slice(h // 2 * 128, (h // 2 + 1) * 128)
            if h % 2:
                qh, kh = jnp.where(low_q, qf, q[:, lanes]), jnp.where(low_k, kf, k[:, lanes])
            else:
                qh, kh = jnp.where(low_q, q[:, lanes], qf), jnp.where(low_k, k[:, lanes], kf)
            scores.append(lax.dot_general(qh, kh, (((1,), (1,)), ((), ())), preferred_element_type=F32))
        for s in scores:
            peak = jnp.max(s, axis=-1, keepdims=True)
            weights.append(jnp.exp2((s - peak) * EXP_SCALE).astype(BF))
        for h, e in zip(heads, weights):
            lanes = slice(h // 2 * 128, (h // 2 + 1) * 128)
            vh = jnp.where(low_k, ones, v[:, lanes]) if h % 2 else jnp.where(low_k, v[:, lanes], ones)
            got.append(jnp.dot(e, vh, preferred_element_type=F32))
        for even, odd in zip(got[::2], got[1::2]):
            num = jnp.where(low_q, even, odd)
            den = pltpu.roll(jnp.where(low_q, odd, even), 64, 1)
            tiles.append(num / den)
    return jnp.concatenate(tiles, axis=1)


def mlp(h, gain, wup, wdown):
    a = layer_norm(h, gain).astype(BF)
    acc = h
    for c in range(0, FF, FCHUNK):
        u = jnp.dot(a, wup[:, c : c + FCHUNK], preferred_element_type=F32)
        g = jax.nn.gelu(u).astype(BF)
        acc = acc + jnp.dot(g, wdown[c : c + FCHUNK, :], preferred_element_type=F32)
    return acc


class Weights:
    def __init__(self, block, sources, buffers, sem):
        self.copies = [
            pltpu.make_async_copy(s.at[block], b, sem.at[i]) for i, (s, b) in enumerate(zip(sources, buffers))
        ]
        for c in self.copies:
            c.start()

    def wait(self, i):
        self.copies[i].wait()


WEIGHT_SCRATCH = [
    pltpu.VMEM((D, 3 * D), BF),
    pltpu.VMEM((D, D), BF),
    pltpu.VMEM((D, FF), BF),
    pltpu.VMEM((FF, D), BF),
    pltpu.SemaphoreType.DMA((4,)),
]


def token_labels(region_ref, half, pick_ref, lane_ref, adds_ref, lab_s, first_row):
    lab_s[...] = jnp.zeros_like(lab_s)
    for row in range(6):
        lab_s[row * LEV : (row + 1) * LEV, 0:COLS] = region_ref[half * 6 + row].astype(F32)
    rows = jnp.dot(pick_ref[...], lab_s[...].astype(BF), preferred_element_type=F32)
    region = jnp.sum(rows * lane_ref[...].astype(F32), axis=-1, keepdims=True)
    lab1 = region * 2 + adds_ref[:, 0:1]
    lab2 = region * 8 + adds_ref[:, 1:2]
    if half == 0:
        lab2 = lab2 + adds_ref[:, 2:3] * first_row
    return lab1, lab2


def piece(row, side):
    start = row * 2 * PIECE + side * PIECE
    return slice(start, start + PIECE)


def grouped(value, rt, side):
    return jnp.concatenate([value[piece(rt * 3 + r, side)] for r in range(3)], axis=0)


def first_kernel(
    x_ref, region_ref, pick_ref, lane_ref, adds_ref, g1_ref, g2_ref, wq_hbm, wp_hbm, wu_hbm, wd_hbm,
    own_ref, up_ref, down_ref, left_ref, right_ref, labs_ref,
    xs, lab_s, wq, wp, wu, wd, sem,
):
    weights = Weights(0, (wq_hbm, wp_hbm, wu_hbm, wd_hbm), (wq, wp, wu, wd), sem)
    first_row = (lax.axis_index("lat") == 0).astype(F32)
    g1, g2 = g1_ref[0:1, :], g2_ref[0:1, :]
    tiles = []
    for half in range(2):
        for n in range(half * 72, half * 72 + 72):
            xs[n * LEV : (n + 1) * LEV, :] = x_ref[n // COLS, n % COLS].astype(F32)
        lab1, lab2 = token_labels(region_ref, half, pick_ref, lane_ref, adds_ref, lab_s, first_row)
        x = xs[half * HALF : (half + 1) * HALF]
        a = layer_norm(x, g1).astype(BF)
        if half == 0:
            weights.wait(0)
        qkv = jnp.dot(a, wq[...], preferred_element_type=F32).astype(BF)
        o = attend(
            qkv[:, :D], qkv[:, D : 2 * D], qkv[:, 2 * D :], query_features(lab1, HALF), key_features(lab1, HALF)
        ).astype(BF)
        if half == 0:
            weights.wait(1)
        h = x + jnp.dot(o, wp[...], preferred_element_type=F32)
        if half == 0:
            weights.wait(2)
            weights.wait(3)
        y = mlp(h, g2, wu, wd)
        order = []
        for i in range(2):
            rt = 2 * half + i
            for side in range(2):
                part = grouped(y, i, side).astype(BF)
                labs_ref[(rt * 2 + side) * GROUP : (rt * 2 + side + 1) * GROUP, :] = jnp.broadcast_to(
                    grouped(lab2, i, side), (GROUP, 128)
                )
                own_ref[rt * 2 + side] = part
                (left_ref, right_ref)[side][rt * GROUP : (rt + 1) * GROUP, :] = part
                if rt == 0:
                    up_ref[side * GROUP : (side + 1) * GROUP, :] = part
                if rt == 3:
                    down_ref[side * GROUP : (side + 1) * GROUP, :] = part
        mine = labs_ref[half * HALF : (half + 1) * HALF, :]
        mine = jnp.concatenate([mine, mine[: 384 - HALF]], axis=0)
        tiles.append(jnp.transpose(mine, (1, 0))[0:8])
    row = lax.broadcasted_iota(jnp.int32, (8, 384), 0)
    tile = jnp.where(row == 0, tiles[0], tiles[1])
    tile = jnp.concatenate([tile, jnp.zeros((8, 128), F32)], axis=1).astype(BF)
    up_ref[PER_RT:, :] = tile
    down_ref[PER_RT:, :] = tile
    left_ref[4 * GROUP :, :] = tile
    right_ref[4 * GROUP :, :] = tile


def columns_of(tile):
    t = jnp.transpose(tile.astype(F32)[:, :384], (1, 0))
    return [t[(g % 4) * GROUP : (g % 4 + 1) * GROUP, g // 4 : g // 4 + 1] for g in range(8)]


def second_body(windows, g1_ref, g2_ref, hbm, out_hbm, scratch, rts):
    wq, wp, wu, wd, sem, o_s, x_s, y_s, out_sem = scratch
    weights = Weights(1, hbm, (wq, wp, wu, wd), sem)
    g1, g2 = g1_ref[1:2, :], g2_ref[1:2, :]
    for index, (own, halo) in enumerate(windows):
        n_own = len(own) * GROUP
        x = jnp.concatenate([s[0].astype(F32) for s in own + halo], axis=0)
        lab = jnp.concatenate([s[1] for s in own + halo], axis=0)
        a = layer_norm(x, g1).astype(BF)
        if index == 0:
            weights.wait(0)
        kv = jnp.dot(a, wq[:, D:], preferred_element_type=F32).astype(BF)
        q = jnp.dot(a[:n_own], wq[:, :D], preferred_element_type=F32).astype(BF)
        o = attend(q, kv[:, :D], kv[:, D:], query_features(lab[:n_own], n_own), key_features(lab, 4 * GROUP))
        for i, s in enumerate(own):
            at, side = s[2]
            for r in range(3):
                rows = piece(at * 3 + r, side)
                o_s[rows, :] = o[i * GROUP + r * PIECE : i * GROUP + (r + 1) * PIECE]
                x_s[rows, :] = x[i * GROUP + r * PIECE : i * GROUP + (r + 1) * PIECE]
    weights.wait(1)
    h = x_s[...] + jnp.dot(o_s[...].astype(BF), wp[...], preferred_element_type=F32)
    weights.wait(2)
    weights.wait(3)
    o_s[...] = mlp(h, g2, wu, wd)
    copies = []
    for i, rt in enumerate(rts):
        for n in range(36):
            t = i * PER_RT + n * LEV
            y_s[i * 3 + n // COLS, n % COLS] = o_s[t : t + LEV, :].astype(BF)
        c = pltpu.make_async_copy(y_s.at[i * 3 : i * 3 + 3], out_hbm.at[rt * 3 : rt * 3 + 3], out_sem.at[i])
        c.start()
        copies.append(c)
    for c in copies:
        c.wait()


def own_labels(lab_ref, rt, side):
    start = (rt * 2 + side) * GROUP
    return lab_ref[start : start + GROUP, 0:1]


def middle_kernel(
    own_ref, lh_ref, rh_ref, lab_ref, g1_ref, g2_ref, wq_hbm, wp_hbm, wu_hbm, wd_hbm, out_hbm, *scratch
):
    windows = []
    for side, halo_ref in enumerate((lh_ref, rh_ref)):
        cols = columns_of(halo_ref[4 * GROUP :, :])
        own = [(own_ref[rt * 2 + side], own_labels(lab_ref, rt, side), (rt - 1, side)) for rt in (1, 2)]
        halo = [(halo_ref[rt * GROUP : (rt + 1) * GROUP, :], cols[rt * 2 + 1 - side]) for rt in (1, 2)]
        windows.append((own, halo))
    second_body(windows, g1_ref, g2_ref, (wq_hbm, wp_hbm, wu_hbm, wd_hbm), out_hbm, scratch, (1, 2))


def edge_kernel(
    out_in, own_ref, above_ref, below_ref, lh_ref, rh_ref, lc_ref, rc_ref, lab_ref, g1_ref, g2_ref,
    wq_hbm, wp_hbm, wu_hbm, wd_hbm, out_hbm, *scratch
):
    windows = []
    for at, (rt, v_ref) in enumerate(((0, above_ref), (3, below_ref))):
        theirs = 3 - rt
        vcols = columns_of(v_ref[PER_RT:, :])
        for side, (h_ref, c_ref) in enumerate(((lh_ref, lc_ref), (rh_ref, rc_ref))):
            hcols = columns_of(h_ref[4 * GROUP :, :])
            ccols = columns_of(c_ref[PER_RT + 8 * at : PER_RT + 8 * at + 8, :])
            own = [(own_ref[rt * 2 + side], own_labels(lab_ref, rt, side), (at, side))]
            halo = [
                (v_ref[side * GROUP : (side + 1) * GROUP, :], vcols[theirs * 2 + side]),
                (h_ref[rt * GROUP : (rt + 1) * GROUP, :], hcols[rt * 2 + 1 - side]),
                (c_ref[at * GROUP : (at + 1) * GROUP, :], ccols[theirs * 2 + 1 - side]),
            ]
            windows.append((own, halo))
    second_body(windows, g1_ref, g2_ref, (wq_hbm, wp_hbm, wu_hbm, wd_hbm), out_hbm, scratch, (0, 3))


SECOND_SCRATCH = WEIGHT_SCRATCH + [
    pltpu.VMEM((HALF, D), F32),
    pltpu.VMEM((HALF, D), F32),
    pltpu.VMEM((6, COLS, LEV, D), BF),
    pltpu.SemaphoreType.DMA((2,)),
]

VM = pl.BlockSpec(memory_space=pltpu.VMEM)
ANY = pl.BlockSpec(memory_space=pl.ANY)


def cost(flops, nbytes):
    return pl.CostEstimate(flops=int(flops), bytes_accessed=int(nbytes), transcendentals=0)


def shift(value, axis, steps):
    count = lax.axis_size(axis)
    return lax.ppermute(value, axis, [(s, (s + steps) % count) for s in range(count)])


def first_call(x, region, norm_gain1, norm_gain2, weights):
    pick, lane, adds = token_tables()
    return pl.pallas_call(
        first_kernel,
        out_shape=(
            jax.ShapeDtypeStruct((8, GROUP, D), BF),
            jax.ShapeDtypeStruct((PER_RT + 8, D), BF),
            jax.ShapeDtypeStruct((PER_RT + 8, D), BF),
            jax.ShapeDtypeStruct((4 * GROUP + 8, D), BF),
            jax.ShapeDtypeStruct((4 * GROUP + 8, D), BF),
            jax.ShapeDtypeStruct((TOKENS, 128), F32),
        ),
        in_specs=[VM] * 7 + [ANY] * 4,
        out_specs=[VM] * 6,
        scratch_shapes=[pltpu.VMEM((TOKENS, D), F32), pltpu.VMEM((128, 128), F32)] + WEIGHT_SCRATCH,
        compiler_params=pltpu.CompilerParams(vmem_limit_bytes=VMEM_LIMIT),
        cost_estimate=cost(4e9, 8e6),
        name="first_block",
    )(x, region, jnp.asarray(pick, BF), jnp.asarray(lane, BF), jnp.asarray(adds), norm_gain1, norm_gain2, *weights)


def second_calls(own, left_halo, right_halo, above, below, left_corner, right_corner, labs, norm_gain1, norm_gain2, weights):
    params = pltpu.CompilerParams(vmem_limit_bytes=VMEM_LIMIT)
    out_shape = jax.ShapeDtypeStruct((ROWS, COLS, LEV, D), BF)
    out = pl.pallas_call(
        middle_kernel,
        out_shape=out_shape,
        in_specs=[VM] * 6 + [ANY] * 4,
        out_specs=ANY,
        scratch_shapes=SECOND_SCRATCH,
        compiler_params=params,
        cost_estimate=cost(2.5e9, 8e6),
        name="second_middle",
    )(own, left_halo, right_halo, labs, norm_gain1, norm_gain2, *weights)
    out = pl.pallas_call(
        edge_kernel,
        out_shape=out_shape,
        in_specs=[ANY] + [VM] * 10 + [ANY] * 4,
        out_specs=ANY,
        scratch_shapes=SECOND_SCRATCH,
        input_output_aliases={0: 0},
        compiler_params=params,
        cost_estimate=cost(2.5e9, 8e6),
        name="second_edge",
    )(out, own, above, below, left_halo, right_halo, left_corner, right_corner, labs, norm_gain1, norm_gain2, *weights)
    return out


def per_device(tokens, region, norm_gain1, qkv_weight, proj_weight, norm_gain2, up_weight, down_weight):
    weights = (qkv_weight, proj_weight, up_weight, down_weight)
    params = pltpu.CompilerParams(vmem_limit_bytes=VMEM_LIMIT)
    own, up, down, left, right, labs = first_call(
        jnp.transpose(tokens, (1, 2, 0, 3)), jnp.transpose(region, (1, 0, 2)), norm_gain1, norm_gain2, weights
    )
    below = shift(up, "lat", -1)
    above = shift(down, "lat", 1)
    right_halo = shift(left, "lon", -1)
    left_halo = shift(right, "lon", 1)
    to_left = jnp.concatenate([above[:GROUP], below[:GROUP], above[PER_RT:], below[PER_RT:]], axis=0)
    to_right = jnp.concatenate([above[GROUP:PER_RT], below[GROUP:PER_RT], above[PER_RT:], below[PER_RT:]], axis=0)
    right_corner = shift(to_left, "lon", -1)
    left_corner = shift(to_right, "lon", 1)

    out = second_calls(own, left_halo, right_halo, above, below, left_corner, right_corner, labs, norm_gain1, norm_gain2, weights)
    return jnp.transpose(out, (2, 0, 1, 3))


def solution(mesh):
    return jax.shard_map(
        per_device,
        mesh=mesh,
        in_specs=(P(None, "lat", "lon", None), P(None, "lat", "lon"), P(), P(), P(), P(), P(), P()),
        out_specs=P(None, "lat", "lon", None),
        check_vma=False,
    )
```

```python
import math

import jax
import jax.numpy as jnp
import numpy as np
from jax import lax
from jax.experimental import pallas as pl
from jax.experimental.pallas import tpu as pltpu
from jax.sharding import PartitionSpec as P

BF = jnp.bfloat16
F32 = jnp.float32
LEV, D, FF, HEADS, HD = 4, 512, 2048, 8, 64
ROWS = COLS = 12
PIECE = 6 * LEV
GROUP = 3 * PIECE
PER_RT = 2 * GROUP
HALF = 2 * PER_RT
TOKENS = 2 * HALF
EPS = 1e-05
BIG = 1e30
EXP_SCALE = math.log2(math.e) / math.sqrt(HD)
VMEM_LIMIT = 40 * 1024 * 1024
FCHUNK = 512
STAGE = 8


def token_tables():
    pick = np.zeros((HALF, 128), np.float32)
    lane = np.zeros((HALF, 128), np.float32)
    for row in range(6):
        for col in range(COLS):
            for level in range(LEV):
                t = (row * COLS + col) * LEV + level
                pick[t, row * LEV + level] = 1.0
                lane[t, col] = 1.0
    level = np.arange(HALF) % LEV
    row = np.arange(HALF) // (COLS * LEV)
    adds = np.zeros((HALF, 128), np.float32)
    adds[:, 0] = level // 2
    adds[:, 1] = 4 * (level == 0) + np.where((level == 1) | (level == 2), 0, 1)
    adds[:, 2] = 2 * (row < 3)
    return pick, lane, adds


def layer_norm(x, gain):
    mean = jnp.mean(x, axis=-1, keepdims=True)
    centered = x - mean
    variance = jnp.mean(centered * centered, axis=-1, keepdims=True)
    return centered * lax.rsqrt(variance + EPS) * gain


def one_hot(labels, rows):
    lane = lax.broadcasted_iota(jnp.int32, (rows, 128), 1) & 63
    return lane.astype(F32) == labels


def query_features(labels, rows):
    return jnp.where(one_hot(labels, rows), -BIG, 0.0).astype(BF)


def key_features(labels, rows):
    return jnp.where(one_hot(labels, rows), 0.0, 1.0).astype(BF)


def low_lanes(rows):
    return lax.broadcasted_iota(jnp.int32, (rows, 128), 1) < 64


def attend(q, k, v, qf, kf):
    m, n = q.shape[0], k.shape[0]
    low_q, low_k = low_lanes(m), low_lanes(n)
    ones = jnp.ones((n, 128), BF)
    tiles = []
    for first in range(0, HEADS, STAGE):
        heads = range(first, first + STAGE)
        scores, weights, got = [], [], []
        for h in heads:
            lanes = slice(h // 2 * 128, (h // 2 + 1) * 128)
            if h % 2:
                qh, kh = jnp.where(low_q, qf, q[:, lanes]), jnp.where(low_k, kf, k[:, lanes])
            else:
                qh, kh = jnp.where(low_q, q[:, lanes], qf), jnp.where(low_k, k[:, lanes], kf)
            scores.append(lax.dot_general(qh, kh, (((1,), (1,)), ((), ())), preferred_element_type=F32))
        for s in scores:
            peak = jnp.max(s, axis=-1, keepdims=True)
            weights.append(jnp.exp2((s - peak) * EXP_SCALE).astype(BF))
        for h, e in zip(heads, weights):
            lanes = slice(h // 2 * 128, (h // 2 + 1) * 128)
            vh = jnp.where(low_k, ones, v[:, lanes]) if h % 2 else jnp.where(low_k, v[:, lanes], ones)
            got.append(jnp.dot(e, vh, preferred_element_type=F32))
        for even, odd in zip(got[::2], got[1::2]):
            num = jnp.where(low_q, even, odd)
            den = pltpu.roll(jnp.where(low_q, odd, even), 64, 1)
            tiles.append(num / den)
    return jnp.concatenate(tiles, axis=1)


def token_labels(region_ref, half, pick_ref, lane_ref, adds_ref, lab_s, first_row):
    lab_s[...] = jnp.zeros_like(lab_s)
    for row in range(6):
        lab_s[row * LEV : (row + 1) * LEV, 0:COLS] = region_ref[half * 6 + row].astype(F32)
    rows = jnp.dot(pick_ref[...], lab_s[...].astype(BF), preferred_element_type=F32)
    region = jnp.sum(rows * lane_ref[...].astype(F32), axis=-1, keepdims=True)
    lab1 = region * 2 + adds_ref[:, 0:1]
    lab2 = region * 8 + adds_ref[:, 1:2]
    if half == 0:
        lab2 = lab2 + adds_ref[:, 2:3] * first_row
    return lab1, lab2


def piece(row, side):
    start = row * 2 * PIECE + side * PIECE
    return slice(start, start + PIECE)


def grouped(value, rt, side):
    return jnp.concatenate([value[piece(rt * 3 + r, side)] for r in range(3)], axis=0)


class Inputs:
    def __init__(self, pairs, sem):
        self.copies = [pltpu.make_async_copy(s, b, sem.at[i]) for i, (s, b) in enumerate(pairs)]
        for c in self.copies:
            c.start()

    def wait(self, *which):
        for i in which:
            self.copies[i].wait()


def mlp_chunks(wu_hbm, wd_hbm, block, wu, wd):
    pairs = []
    for c in range(0, FF, FCHUNK):
        pairs.append((wu_hbm.at[block, :, c : c + FCHUNK], wu.at[:, c : c + FCHUNK]))
        pairs.append((wd_hbm.at[block, c : c + FCHUNK, :], wd.at[c : c + FCHUNK, :]))
    return pairs


N_CHUNK = 2 * (FF // FCHUNK)


def mlp(h, gain, wup, wdown, arrived):
    a = layer_norm(h, gain).astype(BF)
    acc = h
    for i, c in enumerate(range(0, FF, FCHUNK)):
        arrived(2 * i, 2 * i + 1)
        u = jnp.dot(a, wup[:, c : c + FCHUNK], preferred_element_type=F32)
        g = jax.nn.gelu(u).astype(BF)
        acc = acc + jnp.dot(g, wdown[c : c + FCHUNK, :], preferred_element_type=F32)
    return acc


def first_kernel(
    x_hbm, region_ref, pick_ref, lane_ref, adds_ref, g1_ref, g2_ref, wq_hbm, wp_hbm, wu_hbm, wd_hbm,
    up_ref, down_ref, tile_ref, mid_hbm,
    xv, xs, lab_s, labs, wq, wp, wu, wd, sem, mid_sem,
):
    inputs = Inputs(
        [(x_hbm.at[0:6], xv.at[0:6]), (wq_hbm.at[0], wq), (x_hbm.at[6:12], xv.at[6:12]), (wp_hbm.at[0], wp)]
        + mlp_chunks(wu_hbm, wd_hbm, 0, wu, wd),
        sem,
    )
    first_row = (lax.axis_index("lat") == 0).astype(F32)
    g1, g2 = g1_ref[0:1, :], g2_ref[0:1, :]
    tiles = []
    for half in range(2):
        lab1, lab2 = token_labels(region_ref, half, pick_ref, lane_ref, adds_ref, lab_s, first_row)
        inputs.wait(2 * half)
        for n in range(half * 72, half * 72 + 72):
            xs[n * LEV : (n + 1) * LEV, :] = xv[n // COLS, n % COLS].astype(F32)
        rows = slice(half * HALF, (half + 1) * HALF)
        a = layer_norm(xs[rows], g1).astype(BF)
        if half == 0:
            inputs.wait(1)
        qkv = jnp.dot(a, wq[...], preferred_element_type=F32).astype(BF)
        o = attend(
            qkv[:, :D], qkv[:, D : 2 * D], qkv[:, 2 * D :], query_features(lab1, HALF), key_features(lab1, HALF)
        ).astype(BF)
        if half == 0:
            inputs.wait(3)
        xs[rows] = xs[rows] + jnp.dot(o, wp[...], preferred_element_type=F32)
        for i in range(2):
            for side in range(2):
                start = (i * 2 + side) * GROUP
                labs[start : start + GROUP, :] = jnp.broadcast_to(grouped(lab2, i, side), (GROUP, 128))
        tiles.append(jnp.transpose(labs[...], (1, 0))[0:8])
    mid = pltpu.make_async_copy(xs.at[PER_RT : 3 * PER_RT], mid_hbm, mid_sem)
    mid.start()
    row = lax.broadcasted_iota(jnp.int32, (8, 384), 0)
    tile = jnp.where(row == 0, tiles[0], tiles[1])
    tile = jnp.concatenate([tile, jnp.zeros((8, 128), F32)], axis=1).astype(BF)
    tile_ref[...] = tile
    h = jnp.concatenate([xs[0:PER_RT], xs[3 * PER_RT :]], axis=0)
    y = mlp(h, g2, wu, wd, lambda *which: inputs.wait(*[4 + w for w in which]))
    for i, ref in enumerate((up_ref, down_ref)):
        for side in range(2):
            ref[side * GROUP : (side + 1) * GROUP, :] = grouped(y, i, side).astype(BF)
        ref[PER_RT:, :] = tile
    mid.wait()


def middle_mlp_kernel(mid_hbm, tile_ref, g2_ref, wu_hbm, wd_hbm, left_ref, right_ref, mid, wu, wd, sem):
    inputs = Inputs([(mid_hbm, mid)] + mlp_chunks(wu_hbm, wd_hbm, 0, wu, wd), sem)
    inputs.wait(0)
    y = mlp(mid[...], g2_ref[0:1, :], wu, wd, lambda *which: inputs.wait(*[1 + w for w in which]))
    for side, ref in enumerate((left_ref, right_ref)):
        for i in range(2):
            ref[i * GROUP : (i + 1) * GROUP, :] = grouped(y, i, side).astype(BF)
        ref[PER_RT:, :] = tile_ref[...]


def columns_of(tile):
    t = jnp.transpose(tile.astype(F32)[:, :384], (1, 0))
    return [t[(g % 4) * GROUP : (g % 4 + 1) * GROUP, g // 4 : g // 4 + 1] for g in range(8)]


def second_body(arrays, windows_of, g1_ref, g2_ref, hbm, out_hbm, scratch, rts):
    wq, wp, wu, wd, sem, o_s, x_s, y_s, out_sem, *buffers = scratch
    wq_hbm, wp_hbm, wu_hbm, wd_hbm = hbm
    inputs = Inputs(
        list(zip(arrays, buffers))
        + [(wq_hbm.at[1, :, D:], wq.at[:, D:]), (wq_hbm.at[1, :, :D], wq.at[:, :D]), (wp_hbm.at[1], wp)]
        + mlp_chunks(wu_hbm, wd_hbm, 1, wu, wd),
        sem,
    )
    at_weights = len(arrays)
    g1, g2 = g1_ref[1:2, :], g2_ref[1:2, :]
    inputs.wait(*range(at_weights))
    for index, (own, halo) in enumerate(windows_of(*buffers)):
        n_own = len(own) * GROUP
        x = jnp.concatenate([s[0].astype(F32) for s in own + halo], axis=0)
        lab = jnp.concatenate([s[1] for s in own + halo], axis=0)
        a = layer_norm(x, g1).astype(BF)
        if index == 0:
            inputs.wait(at_weights)
        kv = jnp.dot(a, wq[:, D:], preferred_element_type=F32).astype(BF)
        if index == 0:
            inputs.wait(at_weights + 1)
        q = jnp.dot(a[:n_own], wq[:, :D], preferred_element_type=F32).astype(BF)
        o = attend(q, kv[:, :D], kv[:, D:], query_features(lab[:n_own], n_own), key_features(lab, 4 * GROUP))
        for i, s in enumerate(own):
            at, side = s[2]
            for r in range(3):
                rows = piece(at * 3 + r, side)
                o_s[rows, :] = o[i * GROUP + r * PIECE : i * GROUP + (r + 1) * PIECE]
                x_s[rows, :] = x[i * GROUP + r * PIECE : i * GROUP + (r + 1) * PIECE]
    inputs.wait(at_weights + 2)
    h = x_s[...] + jnp.dot(o_s[...].astype(BF), wp[...], preferred_element_type=F32)
    o_s[...] = mlp(h, g2, wu, wd, lambda *which: inputs.wait(*[at_weights + 3 + w for w in which]))
    copies = []
    for i, rt in enumerate(rts):
        for n in range(36):
            t = i * PER_RT + n * LEV
            y_s[i * 3 + n // COLS, n % COLS] = o_s[t : t + LEV, :].astype(BF)
        c = pltpu.make_async_copy(y_s.at[i * 3 : i * 3 + 3], out_hbm.at[rt * 3 : rt * 3 + 3], out_sem.at[i])
        c.start()
        copies.append(c)
    for c in copies:
        c.wait()


def rows_of(ref, i):
    return ref[i * GROUP : (i + 1) * GROUP, :]


def middle_windows(left, right, left_halo, right_halo):
    mine = columns_of(left[PER_RT:, :])
    windows = []
    for side, (own_ref, halo_ref) in enumerate(((left, left_halo), (right, right_halo))):
        theirs = columns_of(halo_ref[PER_RT:, :])
        own = [(rows_of(own_ref, rt - 1), mine[rt * 2 + side], (rt - 1, side)) for rt in (1, 2)]
        halo = [(rows_of(halo_ref, rt - 1), theirs[rt * 2 + 1 - side]) for rt in (1, 2)]
        windows.append((own, halo))
    return windows


def edge_windows(up, down, above, below, left_halo, right_halo):
    mine = columns_of(up[PER_RT:, :])
    beside = []
    for ref in (left_halo, right_halo):
        beside.append([columns_of(ref[4 * GROUP + 8 * i : 4 * GROUP + 8 * i + 8, :]) for i in range(3)])
    windows = []
    for at, (rt, own_ref, v_ref) in enumerate(((0, up, above), (3, down, below))):
        theirs = columns_of(v_ref[PER_RT:, :])
        for side, ref in enumerate((left_halo, right_halo)):
            labels = beside[side]
            own = [(rows_of(own_ref, side), mine[rt * 2 + side], (at, side))]
            halo = [
                (rows_of(v_ref, side), theirs[(3 - rt) * 2 + side]),
                (rows_of(ref, at), labels[0][rt * 2 + 1 - side]),
                (rows_of(ref, 2 + at), labels[1 + at][(3 - rt) * 2 + 1 - side]),
            ]
            windows.append((own, halo))
    return windows


def middle_kernel(a, b, c, d, g1_ref, g2_ref, wq_hbm, wp_hbm, wu_hbm, wd_hbm, out_hbm, *scratch):
    hbm = (wq_hbm, wp_hbm, wu_hbm, wd_hbm)
    second_body((a, b, c, d), middle_windows, g1_ref, g2_ref, hbm, out_hbm, scratch, (1, 2))


def edge_kernel(out_in, a, b, c, d, e, f, g1_ref, g2_ref, wq_hbm, wp_hbm, wu_hbm, wd_hbm, out_hbm, *scratch):
    hbm = (wq_hbm, wp_hbm, wu_hbm, wd_hbm)
    second_body((a, b, c, d, e, f), edge_windows, g1_ref, g2_ref, hbm, out_hbm, scratch, (0, 3))


MLP_SCRATCH = [pltpu.VMEM((D, FF), BF), pltpu.VMEM((FF, D), BF)]
WEIGHT_SCRATCH = [pltpu.VMEM((D, 3 * D), BF), pltpu.VMEM((D, D), BF)] + MLP_SCRATCH


def dma(n):
    return pltpu.SemaphoreType.DMA((n,))


def second_scratch(arrays):
    return (
        WEIGHT_SCRATCH
        + [dma(len(arrays) + 3 + N_CHUNK), pltpu.VMEM((HALF, D), F32), pltpu.VMEM((HALF, D), F32)]
        + [pltpu.VMEM((6, COLS, LEV, D), BF), dma(2)]
        + [pltpu.VMEM(a.shape, BF) for a in arrays]
    )


VM = pl.BlockSpec(memory_space=pltpu.VMEM)
ANY = pl.BlockSpec(memory_space=pl.ANY)
HBM = pl.BlockSpec(memory_space=pltpu.HBM)


def cost(flops, nbytes):
    return pl.CostEstimate(flops=int(flops), bytes_accessed=int(nbytes), transcendentals=0)


def in_hbm(value):
    return pltpu.with_memory_space_constraint(value, pltpu.HBM)


def exchange(to_before, to_after, axis):
    count = lax.axis_size(axis)
    odd = lax.axis_index(axis) % 2 == 1
    even_pairs = [(s, s + 1 - 2 * (s % 2)) for s in range(count)]
    odd_pairs = [(s, (s - 1 + 2 * (s % 2)) % count) for s in range(count)]
    one = lax.ppermute(jnp.where(odd, to_before, to_after), axis, even_pairs)
    two = lax.ppermute(jnp.where(odd, to_after, to_before), axis, odd_pairs)
    return one, two, odd


def sorted_out(one, two, odd):
    return jnp.where(odd, one, two), jnp.where(odd, two, one)


def first_calls(tokens, region, g1, g2, weights):
    pick, lane, adds = token_tables()
    tables = [in_hbm(jnp.asarray(t, d)) for t, d in ((pick, BF), (lane, BF), (adds, F32))]
    params = pltpu.CompilerParams(vmem_limit_bytes=VMEM_LIMIT)
    edge_out = jax.ShapeDtypeStruct((PER_RT + 8, D), BF)
    up, down, tile, mid = pl.pallas_call(
        first_kernel,
        out_shape=(
            edge_out, edge_out, jax.ShapeDtypeStruct((8, D), BF), jax.ShapeDtypeStruct((HALF, D), F32),
        ),
        in_specs=[HBM] + [VM] * 6 + [HBM] * 4,
        out_specs=[VM] * 3 + [ANY],
        scratch_shapes=[
            pltpu.VMEM((ROWS, COLS, LEV, D), BF), pltpu.VMEM((TOKENS, D), F32), pltpu.VMEM((128, 128), F32),
            pltpu.VMEM((384, 128), F32),
        ] + WEIGHT_SCRATCH + [dma(4 + N_CHUNK), pltpu.SemaphoreType.DMA],
        compiler_params=params,
        cost_estimate=cost(4e9, 8e6),
        name="first_block",
    )(tokens, region, *tables, g1, g2, *weights)
    left, right = pl.pallas_call(
        middle_mlp_kernel,
        out_shape=(edge_out, edge_out),
        in_specs=[ANY, VM, VM, HBM, HBM],
        out_specs=[VM] * 2,
        scratch_shapes=[pltpu.VMEM((HALF, D), F32)] + MLP_SCRATCH + [dma(1 + N_CHUNK)],
        compiler_params=params,
        cost_estimate=cost(1.3e9, 5e6),
        name="first_middle",
    )(mid, tile, g2, weights[2], weights[3])
    return up, down, left, right


def second_call(kernel, arrays, g1, g2, weights, out=None, name=None):
    given = () if out is None else (out,)
    return pl.pallas_call(
        kernel,
        out_shape=jax.ShapeDtypeStruct((ROWS, COLS, LEV, D), BF),
        in_specs=[HBM] * len(given) + [ANY] * len(arrays) + [VM] * 2 + [HBM] * 4,
        out_specs=HBM,
        scratch_shapes=second_scratch(arrays),
        input_output_aliases={0: 0} if given else {},
        compiler_params=pltpu.CompilerParams(vmem_limit_bytes=VMEM_LIMIT),
        cost_estimate=cost(2.5e9, 8e6),
        name=name,
    )(*given, *arrays, g1, g2, *weights)


def per_device(tokens, region, norm_gain1, qkv_weight, proj_weight, norm_gain2, up_weight, down_weight):
    weights = [in_hbm(w) for w in (qkv_weight, proj_weight, up_weight, down_weight)]
    g1, g2 = in_hbm(norm_gain1), in_hbm(norm_gain2)
    up, down, left, right = first_calls(
        in_hbm(jnp.transpose(tokens, (1, 2, 0, 3))), in_hbm(jnp.transpose(region, (1, 0, 2))), g1, g2, weights
    )
    one, two, odd = exchange(up, down, "lat")
    left, right, one, two = lax.optimization_barrier((left, right, one, two))
    above, below = sorted_out(one, two, odd)
    left_halo, right_halo = sorted_out(*exchange(left, right, "lon"))

    def edge_of(side):
        rows = slice(side * GROUP, (side + 1) * GROUP)
        tiles = [v[PER_RT:] for v in (up, above, below)]
        return jnp.concatenate([up[rows], down[rows], above[rows], below[rows]] + tiles, axis=0)

    left_edge, right_edge = sorted_out(*exchange(edge_of(0), edge_of(1), "lon"))
    out = second_call(middle_kernel, (left, right, left_halo, right_halo), g1, g2, weights, name="second_middle")
    arrays = (up, down, above, below, left_edge, right_edge)
    out = second_call(edge_kernel, arrays, g1, g2, weights, out, name="second_edge")
    return jnp.transpose(out, (2, 0, 1, 3))


def solution(mesh):
    return jax.shard_map(
        per_device,
        mesh=mesh,
        in_specs=(P(None, "lat", "lon", None), P(None, "lat", "lon"), P(), P(), P(), P(), P(), P()),
        out_specs=P(None, "lat", "lon", None),
        check_vma=False,
    )
```

```python
import math

import jax
import jax.numpy as jnp
import numpy as np
from jax import lax
from jax.experimental import pallas as pl
from jax.experimental.pallas import tpu as pltpu
from jax.sharding import PartitionSpec as P

BF = jnp.bfloat16
F32 = jnp.float32
LEV, D, FF, HEADS, HD = 4, 512, 2048, 8, 64
ROWS = COLS = 12
PIECE = 6 * LEV
GROUP = 3 * PIECE
PER_RT = 2 * GROUP
HALF = 2 * PER_RT
TOKENS = 2 * HALF
EPS = 1e-05
BIG = 1e30
EXP_SCALE = math.log2(math.e) / math.sqrt(HD)
VMEM_LIMIT = 24 * 1024 * 1024
FCHUNK = 512
STAGE = 8


def token_tables():
    pick = np.zeros((HALF, 128), np.float32)
    lane = np.zeros((HALF, 128), np.float32)
    for row in range(6):
        for col in range(COLS):
            for level in range(LEV):
                t = (row * COLS + col) * LEV + level
                pick[t, row * LEV + level] = 1.0
                lane[t, col] = 1.0
    level = np.arange(HALF) % LEV
    row = np.arange(HALF) // (COLS * LEV)
    adds = np.zeros((HALF, 128), np.float32)
    adds[:, 0] = level // 2
    adds[:, 1] = 4 * (level == 0) + np.where((level == 1) | (level == 2), 0, 1)
    adds[:, 2] = 2 * (row < 3)
    return pick, lane, adds


def layer_norm(x, gain):
    mean = jnp.mean(x, axis=-1, keepdims=True)
    centered = x - mean
    variance = jnp.mean(centered * centered, axis=-1, keepdims=True)
    return centered * lax.rsqrt(variance + EPS) * gain


def one_hot(labels, rows):
    lane = lax.broadcasted_iota(jnp.int32, (rows, 128), 1) & 63
    return lane.astype(F32) == labels


def query_features(labels, rows):
    return jnp.where(one_hot(labels, rows), -BIG, 0.0).astype(BF)


def key_features(labels, rows):
    return jnp.where(one_hot(labels, rows), 0.0, 1.0).astype(BF)


def low_lanes(rows):
    return lax.broadcasted_iota(jnp.int32, (rows, 128), 1) < 64


def attend(q, k, v, qf, kf):
    m, n = q.shape[0], k.shape[0]
    low_q, low_k = low_lanes(m), low_lanes(n)
    ones = jnp.ones((n, 128), BF)
    tiles = []
    for first in range(0, HEADS, STAGE):
        heads = range(first, first + STAGE)
        scores, weights, got = [], [], []
        for h in heads:
            lanes = slice(h // 2 * 128, (h // 2 + 1) * 128)
            if h % 2:
                qh, kh = jnp.where(low_q, qf, q[:, lanes]), jnp.where(low_k, kf, k[:, lanes])
            else:
                qh, kh = jnp.where(low_q, q[:, lanes], qf), jnp.where(low_k, k[:, lanes], kf)
            scores.append(lax.dot_general(qh, kh, (((1,), (1,)), ((), ())), preferred_element_type=F32))
        for s in scores:
            peak = jnp.max(s, axis=-1, keepdims=True)
            weights.append(jnp.exp2((s - peak) * EXP_SCALE).astype(BF))
        for h, e in zip(heads, weights):
            lanes = slice(h // 2 * 128, (h // 2 + 1) * 128)
            vh = jnp.where(low_k, ones, v[:, lanes]) if h % 2 else jnp.where(low_k, v[:, lanes], ones)
            got.append(jnp.dot(e, vh, preferred_element_type=F32))
        for even, odd in zip(got[::2], got[1::2]):
            num = jnp.where(low_q, even, odd)
            den = pltpu.roll(jnp.where(low_q, odd, even), 64, 1)
            tiles.append(num / den)
    return jnp.concatenate(tiles, axis=1)


def is_odd(axis):
    return lax.rem(lax.axis_index(axis), 2) == 1


def token_labels(region_ref, half, pick_ref, lane_ref, adds_ref, lab_s, first_row):
    lab_s[...] = jnp.zeros_like(lab_s)
    for row in range(6):
        lab_s[row * LEV : (row + 1) * LEV, 0:COLS] = region_ref[half * 6 + row].astype(F32)
    rows = jnp.dot(pick_ref[...], lab_s[...].astype(BF), preferred_element_type=F32)
    region = jnp.sum(rows * lane_ref[...].astype(F32), axis=-1, keepdims=True)
    lab1 = region * 2 + adds_ref[:, 0:1]
    lab2 = region * 8 + adds_ref[:, 1:2]
    if half == 0:
        lab2 = lab2 + adds_ref[:, 2:3] * first_row
    return lab1, lab2


def piece(row, side):
    start = row * 2 * PIECE + side * PIECE
    return slice(start, start + PIECE)


def grouped(value, rt, side):
    return jnp.concatenate([value[piece(rt * 3 + r, side)] for r in range(3)], axis=0)


class Inputs:
    def __init__(self, pairs, sem):
        self.copies = [pltpu.make_async_copy(s, b, sem.at[i]) for i, (s, b) in enumerate(pairs)]
        for c in self.copies:
            c.start()

    def wait(self, *which):
        for i in which:
            self.copies[i].wait()


def mlp_chunks(wu_hbm, wd_hbm, block, wu, wd):
    pairs = []
    for c in range(0, FF, FCHUNK):
        pairs.append((wu_hbm.at[block, :, c : c + FCHUNK], wu.at[:, c : c + FCHUNK]))
        pairs.append((wd_hbm.at[block, c : c + FCHUNK, :], wd.at[c : c + FCHUNK, :]))
    return pairs


N_CHUNK = 2 * (FF // FCHUNK)


def mlp(h, gain, wup, wdown, arrived):
    a = layer_norm(h, gain).astype(BF)
    acc = h
    for i, c in enumerate(range(0, FF, FCHUNK)):
        arrived(2 * i, 2 * i + 1)
        u = jnp.dot(a, wup[:, c : c + FCHUNK], preferred_element_type=F32)
        g = jax.nn.gelu(u).astype(BF)
        acc = acc + jnp.dot(g, wdown[c : c + FCHUNK, :], preferred_element_type=F32)
    return acc


def first_kernel(
    x_hbm, region_hbm, pick_hbm, lane_hbm, adds_hbm, g1_hbm, g2_hbm, wq_hbm, wp_hbm, wu_hbm, wd_hbm,
    one_ref, two_ref, tile_ref, mid_ref, wu, g1_ref, g2_ref,
    xv, xs, lab_s, labs, region_ref, pick_ref, lane_ref, adds_ref, wq, wp, wd, sem, mlp_sem, small_sem,
):
    small = Inputs(
        [
            (region_hbm, region_ref), (pick_hbm, pick_ref), (lane_hbm, lane_ref), (adds_hbm, adds_ref),
            (g1_hbm, g1_ref), (g2_hbm, g2_ref),
        ],
        small_sem,
    )
    inputs = Inputs(
        [(x_hbm.at[0:6], xv.at[0:6]), (wq_hbm.at[0], wq), (x_hbm.at[6:12], xv.at[6:12]), (wp_hbm.at[0], wp)], sem
    )
    first_row = (lax.axis_index("lat") == 0).astype(F32)
    small.wait(*range(6))
    g1, g2 = g1_ref[0:1, :], g2_ref[0:1, :]
    tiles = []
    for half in range(2):
        lab1, lab2 = token_labels(region_ref, half, pick_ref, lane_ref, adds_ref, lab_s, first_row)
        inputs.wait(2 * half)
        for n in range(half * 72, half * 72 + 72):
            xs[n * LEV : (n + 1) * LEV, :] = xv[n // COLS, n % COLS].astype(F32)
        rows = slice(half * HALF, (half + 1) * HALF)
        a = layer_norm(xs[rows], g1).astype(BF)
        if half == 0:
            inputs.wait(1)
            mlp_inputs = Inputs(mlp_chunks(wu_hbm, wd_hbm, 0, wu, wd), mlp_sem)
        qkv = jnp.dot(a, wq[...], preferred_element_type=F32).astype(BF)
        o = attend(
            qkv[:, :D], qkv[:, D : 2 * D], qkv[:, 2 * D :], query_features(lab1, HALF), key_features(lab1, HALF)
        ).astype(BF)
        if half == 0:
            inputs.wait(3)
        xs[rows] = xs[rows] + jnp.dot(o, wp[...], preferred_element_type=F32)
        for i in range(2):
            for side in range(2):
                start = (i * 2 + side) * GROUP
                labs[start : start + GROUP, :] = jnp.broadcast_to(grouped(lab2, i, side), (GROUP, 128))
        tiles.append(jnp.transpose(labs[...], (1, 0))[0:8])
    mid_ref[...] = xs[PER_RT : 3 * PER_RT]
    row = lax.broadcasted_iota(jnp.int32, (8, 384), 0)
    tile = jnp.where(row == 0, tiles[0], tiles[1])
    tile = jnp.concatenate([tile, jnp.zeros((8, 128), F32)], axis=1).astype(BF)
    tile_ref[...] = tile
    h = jnp.concatenate([xs[0:PER_RT], xs[3 * PER_RT :]], axis=0)
    y = mlp(h, g2, wu, wd, mlp_inputs.wait)
    odd = is_odd("lat")
    for side in range(2):
        rows = slice(side * GROUP, (side + 1) * GROUP)
        up, down = grouped(y, 0, side), grouped(y, 1, side)
        one_ref[rows, :] = jnp.where(odd, up, down).astype(BF)
        two_ref[rows, :] = jnp.where(odd, down, up).astype(BF)
    one_ref[PER_RT:, :] = tile
    two_ref[PER_RT:, :] = tile


def middle_mlp_kernel(mid, tile_ref, g2_ref, wu, wd_hbm, wq_hbm, one_ref, two_ref, wq1, wd, sem):
    chunks = [slice(c, c + FCHUNK) for c in range(0, FF, FCHUNK)]
    inputs = Inputs([(wd_hbm.at[0, c], wd.at[c]) for c in chunks] + [(wq_hbm.at[1], wq1)], sem)
    y = mlp(mid[...], g2_ref[0:1, :], wu, wd, lambda up, down: inputs.wait(down // 2))
    odd = is_odd("lon")
    for i in range(2):
        rows = slice(i * GROUP, (i + 1) * GROUP)
        left, right = grouped(y, i, 0), grouped(y, i, 1)
        one_ref[rows, :] = jnp.where(odd, left, right).astype(BF)
        two_ref[rows, :] = jnp.where(odd, right, left).astype(BF)
    one_ref[PER_RT:, :] = tile_ref[...]
    two_ref[PER_RT:, :] = tile_ref[...]
    inputs.wait(N_CHUNK // 2)


class Either:
    def __init__(self, odd, first, second):
        self.odd, self.first, self.second = odd, first, second

    def __getitem__(self, at):
        return jnp.where(self.odd, self.first[at].astype(F32), self.second[at].astype(F32))


def both_ways(axis, one, two):
    odd = is_odd(axis)
    return Either(odd, one, two), Either(odd, two, one)


def pack_kernel(own_one, own_two, one, two, first_ref, second_ref):
    up, down = both_ways("lat", own_one, own_two)
    above, below = both_ways("lat", one, two)
    odd = is_odd("lon")
    for i, v in enumerate((up, down, above, below)):
        left, right = (v[side * GROUP : (side + 1) * GROUP, :] for side in range(2))
        rows = slice(i * GROUP, (i + 1) * GROUP)
        first_ref[rows, :] = jnp.where(odd, left, right).astype(BF)
        second_ref[rows, :] = jnp.where(odd, right, left).astype(BF)
    for i, v in enumerate((up, above, below)):
        rows = slice(4 * GROUP + 8 * i, 4 * GROUP + 8 * i + 8)
        tile = v[PER_RT:, :].astype(BF)
        first_ref[rows, :] = tile
        second_ref[rows, :] = tile


def columns_of(tile):
    t = jnp.transpose(tile.astype(F32)[:, :384], (1, 0))
    return [t[(g % 4) * GROUP : (g % 4 + 1) * GROUP, g // 4 : g // 4 + 1] for g in range(8)]


def second_body(arrays, windows_of, g1_ref, g2_ref, hbm, weights, out_hbm, scratch, rts):
    o_s, x_s, y_s, out_sem, *sem = scratch
    wq, wp, wu, wd = weights
    arrived = (lambda *which: None) if hbm is None else Inputs(second_copies(hbm, weights), sem[0]).wait
    g1, g2 = g1_ref[1:2, :], g2_ref[1:2, :]
    for own, halo in windows_of(*arrays):
        n_own = len(own) * GROUP
        x = jnp.concatenate([s[0].astype(F32) for s in own + halo], axis=0)
        lab = jnp.concatenate([s[1] for s in own + halo], axis=0)
        a = layer_norm(x, g1).astype(BF)
        kv = jnp.dot(a, wq[:, D:], preferred_element_type=F32).astype(BF)
        q = jnp.dot(a[:n_own], wq[:, :D], preferred_element_type=F32).astype(BF)
        o = attend(q, kv[:, :D], kv[:, D:], query_features(lab[:n_own], n_own), key_features(lab, 4 * GROUP))
        for i, s in enumerate(own):
            at, side = s[2]
            for r in range(3):
                rows = piece(at * 3 + r, side)
                o_s[rows, :] = o[i * GROUP + r * PIECE : i * GROUP + (r + 1) * PIECE]
                x_s[rows, :] = x[i * GROUP + r * PIECE : i * GROUP + (r + 1) * PIECE]
    arrived(0)
    h = x_s[...] + jnp.dot(o_s[...].astype(BF), wp[...], preferred_element_type=F32)
    o_s[...] = mlp(h, g2, wu, wd, lambda *which: arrived(*[1 + w for w in which]))
    copies = []
    for i, rt in enumerate(rts):
        for n in range(36):
            t = i * PER_RT + n * LEV
            y_s[i * 3 + n // COLS, n % COLS] = o_s[t : t + LEV, :].astype(BF)
        c = pltpu.make_async_copy(y_s.at[i * 3 : i * 3 + 3], out_hbm.at[rt * 3 : rt * 3 + 3], out_sem.at[i])
        c.start()
        copies.append(c)
    for c in copies:
        c.wait()


def rows_of(ref, i):
    return ref[i * GROUP : (i + 1) * GROUP, :]


def middle_windows(own_one, own_two, one, two):
    left, right = both_ways("lon", own_one, own_two)
    left_halo, right_halo = both_ways("lon", one, two)
    mine = columns_of(left[PER_RT:, :])
    windows = []
    for side, (own_ref, halo_ref) in enumerate(((left, left_halo), (right, right_halo))):
        theirs = columns_of(halo_ref[PER_RT:, :])
        own = [(rows_of(own_ref, rt - 1), mine[rt * 2 + side], (rt - 1, side)) for rt in (1, 2)]
        halo = [(rows_of(halo_ref, rt - 1), theirs[rt * 2 + 1 - side]) for rt in (1, 2)]
        windows.append((own, halo))
    return windows


def edge_windows(own_one, own_two, v_one, v_two, h_one, h_two):
    up, down = both_ways("lat", own_one, own_two)
    above, below = both_ways("lat", v_one, v_two)
    left_halo, right_halo = both_ways("lon", h_one, h_two)
    mine = columns_of(up[PER_RT:, :])
    beside = []
    for ref in (left_halo, right_halo):
        beside.append([columns_of(ref[4 * GROUP + 8 * i : 4 * GROUP + 8 * i + 8, :]) for i in range(3)])
    windows = []
    for at, (rt, own_ref, v_ref) in enumerate(((0, up, above), (3, down, below))):
        theirs = columns_of(v_ref[PER_RT:, :])
        for side, ref in enumerate((left_halo, right_halo)):
            labels = beside[side]
            own = [(rows_of(own_ref, side), mine[rt * 2 + side], (at, side))]
            halo = [
                (rows_of(v_ref, side), theirs[(3 - rt) * 2 + side]),
                (rows_of(ref, at), labels[0][rt * 2 + 1 - side]),
                (rows_of(ref, 2 + at), labels[1 + at][(3 - rt) * 2 + 1 - side]),
            ]
            windows.append((own, halo))
    return windows


def second_copies(hbm, weights):
    wp_hbm, wu_hbm, wd_hbm = hbm
    wp, wu, wd = weights[1:]
    return [(wp_hbm.at[1], wp)] + mlp_chunks(wu_hbm, wd_hbm, 1, wu, wd)


def middle_kernel(a, b, c, d, g1_ref, g2_ref, wq, wp_hbm, wu_hbm, wd_hbm, out_hbm, wp, wu, wd, *scratch):
    hbm = (wp_hbm, wu_hbm, wd_hbm)
    second_body((a, b, c, d), middle_windows, g1_ref, g2_ref, hbm, (wq, wp, wu, wd), out_hbm, scratch, (1, 2))


def edge_kernel(out_in, a, b, c, d, e, f, g1_ref, g2_ref, wq, wp, wu, wd, out_hbm, *scratch):
    weights = (wq, wp, wu, wd)
    second_body((a, b, c, d, e, f), edge_windows, g1_ref, g2_ref, None, weights, out_hbm, scratch, (0, 3))


WEIGHT_SCRATCH = [pltpu.VMEM((D, 3 * D), BF), pltpu.VMEM((D, D), BF)]


def dma(n):
    return pltpu.SemaphoreType.DMA((n,))


SECOND_SCRATCH = [
    pltpu.VMEM((HALF, D), F32),
    pltpu.VMEM((HALF, D), F32),
    pltpu.VMEM((6, COLS, LEV, D), BF),
    dma(2),
]

VM = pl.BlockSpec(memory_space=pltpu.VMEM)
ANY = pl.BlockSpec(memory_space=pl.ANY)
HBM = pl.BlockSpec(memory_space=pltpu.HBM)


def cost(flops, nbytes):
    return pl.CostEstimate(flops=int(flops), bytes_accessed=int(nbytes), transcendentals=0)


def in_hbm(value):
    return pltpu.with_memory_space_constraint(value, pltpu.HBM)


def exchange(one, two, axis):
    count = lax.axis_size(axis)
    even_pairs = [(s, s + 1 - 2 * (s % 2)) for s in range(count)]
    odd_pairs = [(s, (s - 1 + 2 * (s % 2)) % count) for s in range(count)]
    return lax.ppermute(one, axis, even_pairs), lax.ppermute(two, axis, odd_pairs)


def first_calls(tokens, region, g1, g2, weights):
    pick, lane, adds = token_tables()
    tables = [in_hbm(jnp.asarray(t, d)) for t, d in ((pick, BF), (lane, BF), (adds, F32))]
    params = pltpu.CompilerParams(vmem_limit_bytes=VMEM_LIMIT)
    edge_out = jax.ShapeDtypeStruct((PER_RT + 8, D), BF)
    up, down, tile, mid, wu, g1, g2 = pl.pallas_call(
        first_kernel,
        out_shape=(
            edge_out, edge_out, pltpu.VMEM((8, D), BF), pltpu.VMEM((HALF, D), F32),
            pltpu.VMEM((D, FF), BF), pltpu.VMEM((2, D), F32), pltpu.VMEM((2, D), F32),
        ),
        in_specs=[HBM] * 11,
        out_specs=[VM] * 7,
        scratch_shapes=[
            pltpu.VMEM((ROWS, COLS, LEV, D), BF), pltpu.VMEM((TOKENS, D), F32), pltpu.VMEM((128, 128), F32),
            pltpu.VMEM((384, 128), F32), pltpu.VMEM((ROWS, LEV, COLS), jnp.int32), pltpu.VMEM((HALF, 128), BF),
            pltpu.VMEM((HALF, 128), BF), pltpu.VMEM((HALF, 128), F32),
        ] + WEIGHT_SCRATCH + [pltpu.VMEM((FF, D), BF), dma(4), dma(N_CHUNK), dma(6)],
        compiler_params=params,
        cost_estimate=cost(4e9, 8e6),
        name="first_block",
    )(tokens, region, *tables, g1, g2, *weights)
    left, right, early = pl.pallas_call(
        middle_mlp_kernel,
        out_shape=(edge_out, edge_out, pltpu.VMEM((D, 3 * D), BF)),
        in_specs=[VM] * 4 + [HBM] * 2,
        out_specs=[VM] * 3,
        scratch_shapes=[pltpu.VMEM((FF, D), BF), dma(N_CHUNK // 2 + 1)],
        compiler_params=params,
        cost_estimate=cost(1.3e9, 5e6),
        name="first_middle",
    )(mid, tile, g2, wu, weights[3], weights[0])
    return up, down, left, right, g1, g2, early


def second_calls(middle, edge, g1, g2, early, weights):
    params = pltpu.CompilerParams(vmem_limit_bytes=VMEM_LIMIT)
    out_shape = jax.ShapeDtypeStruct((ROWS, COLS, LEV, D), BF)
    out, *late = pl.pallas_call(
        middle_kernel,
        out_shape=(
            out_shape, pltpu.VMEM((D, D), BF), pltpu.VMEM((D, FF), BF), pltpu.VMEM((FF, D), BF),
        ),
        in_specs=[VM] * 7 + [HBM] * 3,
        out_specs=[HBM] + [VM] * 3,
        scratch_shapes=SECOND_SCRATCH + [dma(1 + N_CHUNK)],
        compiler_params=params,
        cost_estimate=cost(2.5e9, 8e6),
        name="second_middle",
    )(*middle, g1, g2, early, *weights[1:])
    return pl.pallas_call(
        edge_kernel,
        out_shape=out_shape,
        in_specs=[HBM] + [VM] * 12,
        out_specs=HBM,
        scratch_shapes=SECOND_SCRATCH,
        input_output_aliases={0: 0},
        compiler_params=params,
        cost_estimate=cost(2.5e9, 8e6),
        name="second_edge",
    )(out, *edge, g1, g2, early, *late)


def per_device(tokens, region, norm_gain1, qkv_weight, proj_weight, norm_gain2, up_weight, down_weight):
    weights = [in_hbm(w) for w in (qkv_weight, proj_weight, up_weight, down_weight)]
    g1, g2 = in_hbm(norm_gain1), in_hbm(norm_gain2)
    up, down, left, right, g1, g2, early = first_calls(
        in_hbm(jnp.transpose(tokens, (1, 2, 0, 3))), in_hbm(jnp.transpose(region, (1, 0, 2))), g1, g2, weights
    )
    received = exchange(up, down, "lat")
    left, right, above, below = lax.optimization_barrier((left, right, *received))
    halo = exchange(left, right, "lon")
    message = jax.ShapeDtypeStruct((4 * GROUP + 24, D), BF)
    packed = pl.pallas_call(
        pack_kernel,
        out_shape=(message, message),
        in_specs=[VM] * 4,
        out_specs=[VM] * 2,
        compiler_params=pltpu.CompilerParams(vmem_limit_bytes=8 * 1024 * 1024),
        cost_estimate=cost(1e6, 1e6),
        name="pack_edges",
    )(up, down, above, below)
    beside = exchange(*packed, "lon")
    out = second_calls((left, right, *halo), (up, down, above, below, *beside), g1, g2, early, weights)
    return jnp.transpose(out, (2, 0, 1, 3))


def solution(mesh):
    return jax.shard_map(
        per_device,
        mesh=mesh,
        in_specs=(P(None, "lat", "lon", None), P(None, "lat", "lon"), P(), P(), P(), P(), P(), P()),
        out_specs=P(None, "lat", "lon", None),
        check_vma=False,
    )
```

```python
import math

import jax
import jax.numpy as jnp
import numpy as np
from jax import lax
from jax.experimental import pallas as pl
from jax.experimental.pallas import tpu as pltpu
from jax.sharding import PartitionSpec as P

BF = jnp.bfloat16
F32 = jnp.float32
LEV, D, FF, HEADS, HD = 4, 512, 2048, 8, 64
ROWS = COLS = 12
PIECE = 6 * LEV
GROUP = 3 * PIECE
PER_RT = 2 * GROUP
HALF = 2 * PER_RT
TOKENS = 2 * HALF
EPS = 1e-05
BIG = 1e30
EXP_SCALE = math.log2(math.e) / math.sqrt(HD)
VMEM_LIMIT = 24 * 1024 * 1024
FCHUNK = 512
STAGE = 8


def token_tables():
    pick = np.zeros((HALF, 128), np.float32)
    lane = np.zeros((HALF, 128), np.float32)
    for row in range(6):
        for col in range(COLS):
            for level in range(LEV):
                t = (row * COLS + col) * LEV + level
                pick[t, row * LEV + level] = 1.0
                lane[t, col] = 1.0
    level = np.arange(HALF) % LEV
    row = np.arange(HALF) // (COLS * LEV)
    adds = np.zeros((HALF, 128), np.float32)
    adds[:, 0] = level // 2
    adds[:, 1] = 4 * (level == 0) + np.where((level == 1) | (level == 2), 0, 1)
    adds[:, 2] = 2 * (row < 3)
    return pick, lane, adds


def layer_norm(x, gain):
    mean = jnp.mean(x, axis=-1, keepdims=True)
    centered = x - mean
    variance = jnp.mean(centered * centered, axis=-1, keepdims=True)
    return centered * lax.rsqrt(variance + EPS) * gain


def one_hot(labels, rows):
    lane = lax.broadcasted_iota(jnp.int32, (rows, 128), 1) & 63
    return lane.astype(F32) == labels


def query_features(labels, rows):
    return jnp.where(one_hot(labels, rows), -BIG, 0.0).astype(BF)


def key_features(labels, rows):
    return jnp.where(one_hot(labels, rows), 0.0, 1.0).astype(BF)


def low_lanes(rows):
    return lax.broadcasted_iota(jnp.int32, (rows, 128), 1) < 64


def attend(q, k, v, qf, kf):
    m, n = q.shape[0], k.shape[0]
    low_q, low_k = low_lanes(m), low_lanes(n)
    ones = jnp.ones((n, 128), BF)
    tiles = []
    for first in range(0, HEADS, STAGE):
        heads = range(first, first + STAGE)
        scores, weights, got = [], [], []
        for h in heads:
            lanes = slice(h // 2 * 128, (h // 2 + 1) * 128)
            if h % 2:
                qh, kh = jnp.where(low_q, qf, q[:, lanes]), jnp.where(low_k, kf, k[:, lanes])
            else:
                qh, kh = jnp.where(low_q, q[:, lanes], qf), jnp.where(low_k, k[:, lanes], kf)
            scores.append(lax.dot_general(qh, kh, (((1,), (1,)), ((), ())), preferred_element_type=F32))
        for s in scores:
            peak = jnp.max(s, axis=-1, keepdims=True)
            weights.append(jnp.exp2((s - peak) * EXP_SCALE).astype(BF))
        for h, e in zip(heads, weights):
            lanes = slice(h // 2 * 128, (h // 2 + 1) * 128)
            vh = jnp.where(low_k, ones, v[:, lanes]) if h % 2 else jnp.where(low_k, v[:, lanes], ones)
            got.append(jnp.dot(e, vh, preferred_element_type=F32))
        for even, odd in zip(got[::2], got[1::2]):
            num = jnp.where(low_q, even, odd)
            den = pltpu.roll(jnp.where(low_q, odd, even), 64, 1)
            tiles.append(num / den)
    return jnp.concatenate(tiles, axis=1)


def is_odd(axis):
    return lax.rem(lax.axis_index(axis), 2) == 1


def token_labels(region_ref, half, pick_ref, lane_ref, adds_ref, lab_s, first_row):
    lab_s[...] = jnp.zeros_like(lab_s)
    for row in range(6):
        lab_s[row * LEV : (row + 1) * LEV, 0:COLS] = region_ref[half * 6 + row].astype(F32)
    rows = jnp.dot(pick_ref[...], lab_s[...].astype(BF), preferred_element_type=F32)
    region = jnp.sum(rows * lane_ref[...].astype(F32), axis=-1, keepdims=True)
    lab1 = region * 2 + adds_ref[:, 0:1]
    lab2 = region * 8 + adds_ref[:, 1:2]
    if half == 0:
        lab2 = lab2 + adds_ref[:, 2:3] * first_row
    return lab1, lab2


def piece(row, side):
    start = row * 2 * PIECE + side * PIECE
    return slice(start, start + PIECE)


def grouped(value, rt, side):
    return jnp.concatenate([value[piece(rt * 3 + r, side)] for r in range(3)], axis=0)


class Inputs:
    def __init__(self, pairs, sem):
        self.copies = [pltpu.make_async_copy(s, b, sem.at[i]) for i, (s, b) in enumerate(pairs)]
        for c in self.copies:
            c.start()

    def wait(self, *which):
        for i in which:
            self.copies[i].wait()


def mlp_chunks(wu_hbm, wd_hbm, block, wu, wd):
    pairs = []
    for c in range(0, FF, FCHUNK):
        pairs.append((wu_hbm.at[block, :, c : c + FCHUNK], wu.at[:, c : c + FCHUNK]))
        pairs.append((wd_hbm.at[block, c : c + FCHUNK, :], wd.at[c : c + FCHUNK, :]))
    return pairs


N_CHUNK = 2 * (FF // FCHUNK)


def mlp(h, gain, wup, wdown, arrived):
    a = layer_norm(h, gain).astype(BF)
    acc = h
    for i, c in enumerate(range(0, FF, FCHUNK)):
        arrived(2 * i, 2 * i + 1)
        u = jnp.dot(a, wup[:, c : c + FCHUNK], preferred_element_type=F32)
        g = jax.nn.gelu(u).astype(BF)
        acc = acc + jnp.dot(g, wdown[c : c + FCHUNK, :], preferred_element_type=F32)
    return acc


def first_kernel(
    x_hbm, region_hbm, pick_hbm, lane_hbm, adds_hbm, g1_hbm, g2_hbm, wq_hbm, wp_hbm, wu_hbm, wd_hbm,
    one_ref, two_ref, tile_ref, mid_ref, wu, g1_ref, g2_ref,
    xv, xs, lab_s, labs, region_ref, pick_ref, lane_ref, adds_ref, wq, wp, wd, sem, mlp_sem, small_sem,
):
    small = Inputs(
        [
            (region_hbm, region_ref), (pick_hbm, pick_ref), (lane_hbm, lane_ref), (adds_hbm, adds_ref),
            (g1_hbm, g1_ref), (g2_hbm, g2_ref),
        ],
        small_sem,
    )
    inputs = Inputs(
        [(x_hbm.at[0:6], xv.at[0:6]), (wq_hbm.at[0], wq), (x_hbm.at[6:12], xv.at[6:12]), (wp_hbm.at[0], wp)], sem
    )
    first_row = (lax.axis_index("lat") == 0).astype(F32)
    small.wait(*range(6))
    g1, g2 = g1_ref[0:1, :], g2_ref[0:1, :]
    tiles = []
    for half in range(2):
        lab1, lab2 = token_labels(region_ref, half, pick_ref, lane_ref, adds_ref, lab_s, first_row)
        inputs.wait(2 * half)
        for n in range(half * 72, half * 72 + 72):
            xs[n * LEV : (n + 1) * LEV, :] = xv[n // COLS, n % COLS].astype(F32)
        rows = slice(half * HALF, (half + 1) * HALF)
        a = layer_norm(xs[rows], g1).astype(BF)
        if half == 0:
            inputs.wait(1)
            mlp_inputs = Inputs(mlp_chunks(wu_hbm, wd_hbm, 0, wu, wd), mlp_sem)
        qkv = jnp.dot(a, wq[...], preferred_element_type=F32).astype(BF)
        o = attend(
            qkv[:, :D], qkv[:, D : 2 * D], qkv[:, 2 * D :], query_features(lab1, HALF), key_features(lab1, HALF)
        ).astype(BF)
        if half == 0:
            inputs.wait(3)
        xs[rows] = xs[rows] + jnp.dot(o, wp[...], preferred_element_type=F32)
        for i in range(2):
            for side in range(2):
                start = (i * 2 + side) * GROUP
                labs[start : start + GROUP, :] = jnp.broadcast_to(grouped(lab2, i, side), (GROUP, 128))
        tiles.append(jnp.transpose(labs[...], (1, 0))[0:8])
    mid_ref[...] = xs[PER_RT : 3 * PER_RT]
    row = lax.broadcasted_iota(jnp.int32, (8, 384), 0)
    tile = jnp.where(row == 0, tiles[0], tiles[1])
    tile = jnp.concatenate([tile, jnp.zeros((8, 128), F32)], axis=1).astype(BF)
    tile_ref[...] = tile
    h = jnp.concatenate([xs[0:PER_RT], xs[3 * PER_RT :]], axis=0)
    y = mlp(h, g2, wu, wd, mlp_inputs.wait)
    odd = is_odd("lat")
    for side in range(2):
        rows = slice(side * GROUP, (side + 1) * GROUP)
        up, down = grouped(y, 0, side), grouped(y, 1, side)
        one_ref[rows, :] = jnp.where(odd, up, down).astype(BF)
        two_ref[rows, :] = jnp.where(odd, down, up).astype(BF)
    one_ref[PER_RT:, :] = tile
    two_ref[PER_RT:, :] = tile


def middle_mlp_kernel(mid, tile_ref, g2_ref, wu, wd_hbm, wq_hbm, one_ref, two_ref, wq1, wd, sem):
    chunks = [slice(c, c + FCHUNK) for c in range(0, FF, FCHUNK)]
    inputs = Inputs([(wd_hbm.at[0, c], wd.at[c]) for c in chunks] + [(wq_hbm.at[1], wq1)], sem)
    y = mlp(mid[...], g2_ref[0:1, :], wu, wd, lambda up, down: inputs.wait(down // 2))
    odd = is_odd("lon")
    for i in range(2):
        rows = slice(i * GROUP, (i + 1) * GROUP)
        left, right = grouped(y, i, 0), grouped(y, i, 1)
        one_ref[rows, :] = jnp.where(odd, left, right).astype(BF)
        two_ref[rows, :] = jnp.where(odd, right, left).astype(BF)
    one_ref[PER_RT:, :] = tile_ref[...]
    two_ref[PER_RT:, :] = tile_ref[...]
    inputs.wait(N_CHUNK // 2)


class Either:
    def __init__(self, odd, first, second):
        self.odd, self.first, self.second = odd, first, second

    def __getitem__(self, at):
        return jnp.where(self.odd, self.first[at].astype(F32), self.second[at].astype(F32))


def both_ways(axis, one, two):
    odd = is_odd(axis)
    return Either(odd, one, two), Either(odd, two, one)


def pack_kernel(own_one, own_two, one, two, first_ref, second_ref):
    up, down = both_ways("lat", own_one, own_two)
    above, below = both_ways("lat", one, two)
    odd = is_odd("lon")
    for i, v in enumerate((up, down, above, below)):
        left, right = (v[side * GROUP : (side + 1) * GROUP, :] for side in range(2))
        rows = slice(i * GROUP, (i + 1) * GROUP)
        first_ref[rows, :] = jnp.where(odd, left, right).astype(BF)
        second_ref[rows, :] = jnp.where(odd, right, left).astype(BF)
    for i, v in enumerate((up, above, below)):
        rows = slice(4 * GROUP + 8 * i, 4 * GROUP + 8 * i + 8)
        tile = v[PER_RT:, :].astype(BF)
        first_ref[rows, :] = tile
        second_ref[rows, :] = tile


def columns_of(tile):
    t = jnp.transpose(tile.astype(F32)[:, :384], (1, 0))
    return [t[(g % 4) * GROUP : (g % 4 + 1) * GROUP, g // 4 : g // 4 + 1] for g in range(8)]


def second_body(arrays, windows_of, g1_ref, g2_ref, hbm, weights, out_hbm, scratch, rts):
    o_s, x_s, y_s, out_sem, *sem = scratch
    wq, wp, wu, wd = weights
    arrived = (lambda *which: None) if hbm is None else Inputs(second_copies(hbm, weights), sem[0]).wait
    g1, g2 = g1_ref[1:2, :], g2_ref[1:2, :]
    for own, halo in windows_of(*arrays):
        n_own = len(own) * GROUP
        x = jnp.concatenate([s[0].astype(F32) for s in own + halo], axis=0)
        lab = jnp.concatenate([s[1] for s in own + halo], axis=0)
        a = layer_norm(x, g1).astype(BF)
        kv = jnp.dot(a, wq[:, D:], preferred_element_type=F32).astype(BF)
        q = jnp.dot(a[:n_own], wq[:, :D], preferred_element_type=F32).astype(BF)
        o = attend(q, kv[:, :D], kv[:, D:], query_features(lab[:n_own], n_own), key_features(lab, 4 * GROUP))
        for i, s in enumerate(own):
            at, side = s[2]
            for r in range(3):
                rows = piece(at * 3 + r, side)
                o_s[rows, :] = o[i * GROUP + r * PIECE : i * GROUP + (r + 1) * PIECE]
                x_s[rows, :] = x[i * GROUP + r * PIECE : i * GROUP + (r + 1) * PIECE]
    arrived(0)
    h = x_s[...] + jnp.dot(o_s[...].astype(BF), wp[...], preferred_element_type=F32)
    o_s[...] = mlp(h, g2, wu, wd, lambda *which: arrived(*[1 + w for w in which]))
    copies = []
    for i, rt in enumerate(rts):
        for n in range(36):
            t = i * PER_RT + n * LEV
            y_s[i * 3 + n // COLS, n % COLS] = o_s[t : t + LEV, :].astype(BF)
        c = pltpu.make_async_copy(y_s.at[i * 3 : i * 3 + 3], out_hbm.at[rt * 3 : rt * 3 + 3], out_sem.at[i])
        c.start()
        copies.append(c)
    for c in copies:
        c.wait()


def rows_of(ref, i):
    return ref[i * GROUP : (i + 1) * GROUP, :]


def middle_windows(own_one, own_two, one, two):
    left, right = both_ways("lon", own_one, own_two)
    left_halo, right_halo = both_ways("lon", one, two)
    mine = columns_of(left[PER_RT:, :])
    windows = []
    for side, (own_ref, halo_ref) in enumerate(((left, left_halo), (right, right_halo))):
        theirs = columns_of(halo_ref[PER_RT:, :])
        own = [(rows_of(own_ref, rt - 1), mine[rt * 2 + side], (rt - 1, side)) for rt in (1, 2)]
        halo = [(rows_of(halo_ref, rt - 1), theirs[rt * 2 + 1 - side]) for rt in (1, 2)]
        windows.append((own, halo))
    return windows


def edge_windows(own_one, own_two, v_one, v_two, h_one, h_two):
    up, down = both_ways("lat", own_one, own_two)
    above, below = both_ways("lat", v_one, v_two)
    left_halo, right_halo = both_ways("lon", h_one, h_two)
    mine = columns_of(up[PER_RT:, :])
    beside = []
    for ref in (left_halo, right_halo):
        beside.append([columns_of(ref[4 * GROUP + 8 * i : 4 * GROUP + 8 * i + 8, :]) for i in range(3)])
    windows = []
    for at, (rt, own_ref, v_ref) in enumerate(((0, up, above), (3, down, below))):
        theirs = columns_of(v_ref[PER_RT:, :])
        for side, ref in enumerate((left_halo, right_halo)):
            labels = beside[side]
            own = [(rows_of(own_ref, side), mine[rt * 2 + side], (at, side))]
            halo = [
                (rows_of(v_ref, side), theirs[(3 - rt) * 2 + side]),
                (rows_of(ref, at), labels[0][rt * 2 + 1 - side]),
                (rows_of(ref, 2 + at), labels[1 + at][(3 - rt) * 2 + 1 - side]),
            ]
            windows.append((own, halo))
    return windows


def second_copies(hbm, weights):
    wp_hbm, wu_hbm, wd_hbm = hbm
    wp, wu, wd = weights[1:]
    return [(wp_hbm.at[1], wp)] + mlp_chunks(wu_hbm, wd_hbm, 1, wu, wd)


def middle_kernel(a, b, c, d, g1_ref, g2_ref, wq, wp_hbm, wu_hbm, wd_hbm, out_hbm, wp, wu, wd, *scratch):
    hbm = (wp_hbm, wu_hbm, wd_hbm)
    second_body((a, b, c, d), middle_windows, g1_ref, g2_ref, hbm, (wq, wp, wu, wd), out_hbm, scratch, (1, 2))


def edge_kernel(out_in, a, b, c, d, e, f, g1_ref, g2_ref, wq, wp, wu, wd, out_hbm, *scratch):
    weights = (wq, wp, wu, wd)
    second_body((a, b, c, d, e, f), edge_windows, g1_ref, g2_ref, None, weights, out_hbm, scratch, (0, 3))


WEIGHT_SCRATCH = [pltpu.VMEM((D, 3 * D), BF), pltpu.VMEM((D, D), BF)]


def dma(n):
    return pltpu.SemaphoreType.DMA((n,))


SECOND_SCRATCH = [
    pltpu.VMEM((HALF, D), F32),
    pltpu.VMEM((HALF, D), F32),
    pltpu.VMEM((6, COLS, LEV, D), BF),
    dma(2),
]

VM = pl.BlockSpec(memory_space=pltpu.VMEM)
ANY = pl.BlockSpec(memory_space=pl.ANY)
HBM = pl.BlockSpec(memory_space=pltpu.HBM)


def cost(flops, nbytes):
    return pl.CostEstimate(flops=int(flops), bytes_accessed=int(nbytes), transcendentals=0)


def in_hbm(value):
    return pltpu.with_memory_space_constraint(value, pltpu.HBM)


def exchange(one, two, axis):
    count = lax.axis_size(axis)
    even_pairs = [(s, s + 1 - 2 * (s % 2)) for s in range(count)]
    odd_pairs = [(s, (s - 1 + 2 * (s % 2)) % count) for s in range(count)]
    return lax.ppermute(one, axis, even_pairs), lax.ppermute(two, axis, odd_pairs)


def first_calls(tokens, region, g1, g2, weights):
    pick, lane, adds = token_tables()
    tables = [in_hbm(jnp.asarray(t, d)) for t, d in ((pick, BF), (lane, BF), (adds, F32))]
    params = pltpu.CompilerParams(vmem_limit_bytes=VMEM_LIMIT)
    edge_out = jax.ShapeDtypeStruct((PER_RT + 8, D), BF)
    up, down, tile, mid, wu, g1, g2 = pl.pallas_call(
        first_kernel,
        out_shape=(
            edge_out, edge_out, pltpu.VMEM((8, D), BF), pltpu.VMEM((HALF, D), F32),
            pltpu.VMEM((D, FF), BF), pltpu.VMEM((2, D), F32), pltpu.VMEM((2, D), F32),
        ),
        in_specs=[HBM] * 11,
        out_specs=[VM] * 7,
        scratch_shapes=[
            pltpu.VMEM((ROWS, COLS, LEV, D), BF), pltpu.VMEM((TOKENS, D), F32), pltpu.VMEM((128, 128), F32),
            pltpu.VMEM((384, 128), F32), pltpu.VMEM((ROWS, LEV, COLS), jnp.int32), pltpu.VMEM((HALF, 128), BF),
            pltpu.VMEM((HALF, 128), BF), pltpu.VMEM((HALF, 128), F32),
        ] + WEIGHT_SCRATCH + [pltpu.VMEM((FF, D), BF), dma(4), dma(N_CHUNK), dma(6)],
        compiler_params=params,
        cost_estimate=cost(4e9, 8e6),
        name="first_block",
    )(tokens, region, *tables, g1, g2, *weights)
    left, right, early = pl.pallas_call(
        middle_mlp_kernel,
        out_shape=(edge_out, edge_out, pltpu.VMEM((D, 3 * D), BF)),
        in_specs=[VM] * 4 + [HBM] * 2,
        out_specs=[VM] * 3,
        scratch_shapes=[pltpu.VMEM((FF, D), BF), dma(N_CHUNK // 2 + 1)],
        compiler_params=params,
        cost_estimate=cost(1.3e9, 5e6),
        name="first_middle",
    )(mid, tile, g2, wu, weights[3], weights[0])
    return up, down, left, right, g1, g2, early


def second_calls(middle, edge, g1, g2, early, weights):
    params = pltpu.CompilerParams(vmem_limit_bytes=VMEM_LIMIT)
    out_shape = jax.ShapeDtypeStruct((ROWS, COLS, LEV, D), BF)
    out, *late = pl.pallas_call(
        middle_kernel,
        out_shape=(
            out_shape, pltpu.VMEM((D, D), BF), pltpu.VMEM((D, FF), BF), pltpu.VMEM((FF, D), BF),
        ),
        in_specs=[VM] * 7 + [HBM] * 3,
        out_specs=[HBM] + [VM] * 3,
        scratch_shapes=SECOND_SCRATCH + [dma(1 + N_CHUNK)],
        compiler_params=params,
        cost_estimate=cost(2.5e9, 8e6),
        name="second_middle",
    )(*middle, g1, g2, early, *weights[1:])
    return pl.pallas_call(
        edge_kernel,
        out_shape=out_shape,
        in_specs=[HBM] + [VM] * 12,
        out_specs=HBM,
        scratch_shapes=SECOND_SCRATCH,
        input_output_aliases={0: 0},
        compiler_params=params,
        cost_estimate=cost(2.5e9, 8e6),
        name="second_edge",
    )(out, *edge, g1, g2, early, *late)


def per_device(tokens, region, norm_gain1, qkv_weight, proj_weight, norm_gain2, up_weight, down_weight):
    weights = [in_hbm(w) for w in (qkv_weight, proj_weight, up_weight, down_weight)]
    g1, g2 = in_hbm(norm_gain1), in_hbm(norm_gain2)
    up, down, left, right, g1, g2, early = first_calls(
        in_hbm(jnp.transpose(tokens, (1, 2, 0, 3))), in_hbm(jnp.transpose(region, (1, 0, 2))), g1, g2, weights
    )
    received = exchange(up, down, "lat")
    above, below = received
    left, right, above = lax.optimization_barrier((left, right, above))
    halo = exchange(left, right, "lon")
    message = jax.ShapeDtypeStruct((4 * GROUP + 24, D), BF)
    packed = pl.pallas_call(
        pack_kernel,
        out_shape=(message, message),
        in_specs=[VM] * 4,
        out_specs=[VM] * 2,
        compiler_params=pltpu.CompilerParams(vmem_limit_bytes=8 * 1024 * 1024),
        cost_estimate=cost(1e6, 1e6),
        name="pack_edges",
    )(up, down, above, below)
    beside = exchange(*packed, "lon")
    out = second_calls((left, right, *halo), (up, down, above, below, *beside), g1, g2, early, weights)
    return jnp.transpose(out, (2, 0, 1, 3))


def solution(mesh):
    return jax.shard_map(
        per_device,
        mesh=mesh,
        in_specs=(P(None, "lat", "lon", None), P(None, "lat", "lon"), P(), P(), P(), P(), P(), P()),
        out_specs=P(None, "lat", "lon", None),
        check_vma=False,
    )
```

```python
import math

import jax
import jax.numpy as jnp
import numpy as np
from jax import lax
from jax.experimental import pallas as pl
from jax.experimental.pallas import tpu as pltpu
from jax.sharding import PartitionSpec as P

BF = jnp.bfloat16
F32 = jnp.float32
LEV, D, FF, HEADS, HD = 4, 512, 2048, 8, 64
ROWS = COLS = 12
PIECE = 6 * LEV
GROUP = 3 * PIECE
PER_RT = 2 * GROUP
HALF = 2 * PER_RT
TOKENS = 2 * HALF
EPS = 1e-05
BIG = 1e30
EXP_SCALE = math.log2(math.e) / math.sqrt(HD)
VMEM_LIMIT = 24 * 1024 * 1024
FCHUNK = 1024
PER_LEVEL = HALF // LEV


def token_tables():
    pick = np.zeros((HALF, 128), np.float32)
    lane = np.zeros((HALF, 128), np.float32)
    for row in range(6):
        for col in range(COLS):
            for level in range(LEV):
                t = (row * COLS + col) * LEV + level
                pick[t, row * LEV + level] = 1.0
                lane[t, col] = 1.0
    level = np.arange(HALF) % LEV
    row = np.arange(HALF) // (COLS * LEV)
    adds = np.zeros((HALF, 128), np.float32)
    adds[:, 1] = 4 * (level == 0) + np.where((level == 1) | (level == 2), 0, 1)
    adds[:, 2] = 2 * (row < 3)
    return pick, lane, adds


def layer_norm(x, gain):
    mean = jnp.mean(x, axis=-1, keepdims=True)
    centered = x - mean
    variance = jnp.mean(centered * centered, axis=-1, keepdims=True)
    return centered * lax.rsqrt(variance + EPS) * gain


def one_hot(labels, rows):
    lane = lax.broadcasted_iota(jnp.int32, (rows, 128), 1) & 63
    return lane.astype(F32) == labels


def query_features(labels, rows):
    return jnp.where(one_hot(labels, rows), -BIG, 0.0).astype(BF)


def key_features(labels, rows):
    return jnp.where(one_hot(labels, rows), 0.0, 1.0).astype(BF)


def low_lanes(rows):
    return lax.broadcasted_iota(jnp.int32, (rows, 128), 1) < 64


def attend_all(parts):
    jobs = [(part, h) for part in parts for h in range(HEADS)]
    scores, weights, got = [], [], []
    for (q, k, v, qf, kf), h in jobs:
        lanes = slice(h // 2 * 128, (h // 2 + 1) * 128)
        low_q, low_k = low_lanes(q.shape[0]), low_lanes(k.shape[0])
        if h % 2:
            qh, kh = jnp.where(low_q, qf, q[:, lanes]), jnp.where(low_k, kf, k[:, lanes])
        else:
            qh, kh = jnp.where(low_q, q[:, lanes], qf), jnp.where(low_k, k[:, lanes], kf)
        scores.append(lax.dot_general(qh, kh, (((1,), (1,)), ((), ())), preferred_element_type=F32))
    for s in scores:
        peak = jnp.max(s, axis=-1, keepdims=True)
        weights.append(jnp.exp2((s - peak) * EXP_SCALE).astype(BF))
    for ((q, k, v, qf, kf), h), e in zip(jobs, weights):
        lanes = slice(h // 2 * 128, (h // 2 + 1) * 128)
        low_k, ones = low_lanes(k.shape[0]), jnp.ones((k.shape[0], 128), BF)
        vh = jnp.where(low_k, ones, v[:, lanes]) if h % 2 else jnp.where(low_k, v[:, lanes], ones)
        got.append(jnp.dot(e, vh, preferred_element_type=F32))
    outs = []
    for i, part in enumerate(parts):
        low_q = low_lanes(part[0].shape[0])
        tiles = []
        for even, odd in zip(got[i * HEADS : (i + 1) * HEADS : 2], got[i * HEADS + 1 : (i + 1) * HEADS : 2]):
            num = jnp.where(low_q, even, odd)
            den = pltpu.roll(jnp.where(low_q, odd, even), 64, 1)
            tiles.append(num / den)
        outs.append(jnp.concatenate(tiles, axis=1))
    return outs


def attend(*part):
    return attend_all([part])[0]


def is_odd(axis):
    return lax.rem(lax.axis_index(axis), 2) == 1


def token_labels(region_ref, half, pick_ref, lane_ref, adds_ref, lab_s, first_row):
    lab_s[0:128, :] = jnp.zeros((128, 128), F32)
    for row in range(6):
        lab_s[row * LEV : (row + 1) * LEV, 0:COLS] = region_ref[half * 6 + row].astype(F32)
    rows = jnp.dot(pick_ref[...], lab_s[0:128, :].astype(BF), preferred_element_type=F32)
    region = jnp.sum(rows * lane_ref[...].astype(F32), axis=-1, keepdims=True)
    lab2 = region * 8 + adds_ref[:, 1:2]
    if half == 0:
        lab2 = lab2 + adds_ref[:, 2:3] * first_row
    lab_s[...] = jnp.broadcast_to(region, (HALF, 128))
    lab1 = jnp.concatenate([lab_s[pl.ds(level, PER_LEVEL, stride=LEV), :] for level in range(LEV)], axis=0)[:, 0:1]
    return lab1, lab2


def load_rows(ref, rows):
    return jnp.concatenate([ref[j, rows, :] for j in range(D // 128)], axis=1)


def store_rows(ref, rows, value):
    for j in range(D // 128):
        ref[j, rows, :] = value[:, j * 128 : (j + 1) * 128]


def piece(row, side):
    start = row * 2 * PIECE + side * PIECE
    return slice(start, start + PIECE)


def grouped(value, rt, side):
    return jnp.concatenate([value[piece(rt * 3 + r, side)] for r in range(3)], axis=0)


class Inputs:
    def __init__(self, pairs, sem):
        self.copies = [pltpu.make_async_copy(s, b, sem.at[i]) for i, (s, b) in enumerate(pairs)]
        for c in self.copies:
            c.start()

    def wait(self, *which):
        for i in which:
            self.copies[i].wait()


def mlp_chunks(wu_hbm, wd_hbm, block, wu, wd):
    pairs = []
    for c in range(0, FF, FCHUNK):
        pairs.append((wu_hbm.at[block, :, c : c + FCHUNK], wu.at[:, c : c + FCHUNK]))
        pairs.append((wd_hbm.at[block, c : c + FCHUNK, :], wd.at[c : c + FCHUNK, :]))
    return pairs


N_CHUNK = 2 * (FF // FCHUNK)


def mlp(h, gain, wup, wdown, arrived):
    a = layer_norm(h, gain).astype(BF)
    acc = h
    for i, c in enumerate(range(0, FF, FCHUNK)):
        arrived(2 * i, 2 * i + 1)
        u = jnp.dot(a, wup[:, c : c + FCHUNK], preferred_element_type=F32)
        g = jax.nn.gelu(u).astype(BF)
        acc = acc + jnp.dot(g, wdown[c : c + FCHUNK, :], preferred_element_type=F32)
    return acc


def first_kernel(
    x_hbm, region_hbm, pick_hbm, lane_hbm, adds_hbm, g1_hbm, g2_hbm, wq_hbm, wp_hbm, wu_hbm, wd_hbm,
    one_ref, two_ref, tile_ref, mid_ref, wu, g1_ref, g2_ref,
    xv, xs, lab_s, labs, region_ref, pick_ref, lane_ref, adds_ref, wq, wp, wd, sem, mlp_sem, small_sem,
):
    small = Inputs(
        [
            (region_hbm, region_ref), (pick_hbm, pick_ref), (lane_hbm, lane_ref), (adds_hbm, adds_ref),
            (g1_hbm, g1_ref), (g2_hbm, g2_ref),
        ],
        small_sem,
    )
    inputs = Inputs(
        [(x_hbm.at[0:6], xv.at[0:6]), (wq_hbm.at[0], wq), (x_hbm.at[6:12], xv.at[6:12]), (wp_hbm.at[0], wp)], sem
    )
    first_row = (lax.axis_index("lat") == 0).astype(F32)
    small.wait(*range(6))
    g1, g2 = g1_ref[0:1, :], g2_ref[0:1, :]
    tiles, features, strides = [], [], []
    for half in range(2):
        lab1, lab2 = token_labels(region_ref, half, pick_ref, lane_ref, adds_ref, lab_s, first_row)
        features += [(query_features(lab1[p], 144), key_features(lab1[p], 144)) for p in (slice(0, 144), slice(144, 288))]
        for i in range(2):
            for side in range(2):
                start = (i * 2 + side) * GROUP
                labs[start : start + GROUP, :] = jnp.broadcast_to(grouped(lab2, i, side), (GROUP, 128))
        tiles.append(jnp.transpose(labs[...], (1, 0))[0:8])
    for half in range(2):
        inputs.wait(2 * half)
        for n in range(half * 72, half * 72 + 72):
            store_rows(xs, slice(n * LEV, (n + 1) * LEV), xv[n // COLS, n % COLS].astype(F32))
        strides += [pl.ds(half * HALF + level, PER_LEVEL, stride=LEV) for level in range(LEV)]
    x = jnp.concatenate([load_rows(xs, rows) for rows in strides], axis=0)
    a = layer_norm(x, g1).astype(BF)
    inputs.wait(1)
    mlp_inputs = Inputs(mlp_chunks(wu_hbm, wd_hbm, 0, wu, wd), mlp_sem)
    qkv = jnp.dot(a, wq[...], preferred_element_type=F32).astype(BF)
    parts = []
    for i, (qf, kf) in enumerate(features):
        p = slice(i * 144, (i + 1) * 144)
        parts.append((qkv[p, :D], qkv[p, D : 2 * D], qkv[p, 2 * D :], qf, kf))
    o = jnp.concatenate(attend_all(parts), axis=0).astype(BF)
    inputs.wait(3)
    h = x + jnp.dot(o, wp[...], preferred_element_type=F32)
    for i, rows in enumerate(strides):
        store_rows(xs, rows, h[i * PER_LEVEL : (i + 1) * PER_LEVEL])
    mid_ref[...] = load_rows(xs, slice(PER_RT, 3 * PER_RT))
    row = lax.broadcasted_iota(jnp.int32, (8, 384), 0)
    tile = jnp.where(row == 0, tiles[0], tiles[1])
    tile = jnp.concatenate([tile, jnp.zeros((8, 128), F32)], axis=1).astype(BF)
    tile_ref[...] = tile
    h = jnp.concatenate([load_rows(xs, slice(0, PER_RT)), load_rows(xs, slice(3 * PER_RT, TOKENS))], axis=0)
    y = mlp(h, g2, wu, wd, mlp_inputs.wait)
    odd = is_odd("lat")
    for side in range(2):
        rows = slice(side * GROUP, (side + 1) * GROUP)
        up, down = grouped(y, 0, side), grouped(y, 1, side)
        one_ref[rows, :] = jnp.where(odd, up, down).astype(BF)
        two_ref[rows, :] = jnp.where(odd, down, up).astype(BF)
    one_ref[PER_RT:, :] = tile
    two_ref[PER_RT:, :] = tile


def middle_mlp_kernel(mid, tile_ref, g2_ref, wu, wd_hbm, wq_hbm, one_ref, two_ref, wq1, wd, sem):
    chunks = [slice(c, c + FCHUNK) for c in range(0, FF, FCHUNK)]
    inputs = Inputs([(wd_hbm.at[0, c], wd.at[c]) for c in chunks] + [(wq_hbm.at[1], wq1)], sem)
    y = mlp(mid[...], g2_ref[0:1, :], wu, wd, lambda up, down: inputs.wait(down // 2))
    odd = is_odd("lon")
    for i in range(2):
        rows = slice(i * GROUP, (i + 1) * GROUP)
        left, right = grouped(y, i, 0), grouped(y, i, 1)
        one_ref[rows, :] = jnp.where(odd, left, right).astype(BF)
        two_ref[rows, :] = jnp.where(odd, right, left).astype(BF)
    one_ref[PER_RT:, :] = tile_ref[...]
    two_ref[PER_RT:, :] = tile_ref[...]
    inputs.wait(N_CHUNK // 2)


class Either:
    def __init__(self, odd, first, second):
        self.odd, self.first, self.second = odd, first, second

    def __getitem__(self, at):
        return jnp.where(self.odd, self.first[at].astype(F32), self.second[at].astype(F32))


def both_ways(axis, one, two):
    odd = is_odd(axis)
    return Either(odd, one, two), Either(odd, two, one)


def pack_kernel(own_one, own_two, one, two, first_ref, second_ref):
    up, down = both_ways("lat", own_one, own_two)
    above, below = both_ways("lat", one, two)
    odd = is_odd("lon")
    for i, v in enumerate((up, down, above, below)):
        left, right = (v[side * GROUP : (side + 1) * GROUP, :] for side in range(2))
        rows = slice(i * GROUP, (i + 1) * GROUP)
        first_ref[rows, :] = jnp.where(odd, left, right).astype(BF)
        second_ref[rows, :] = jnp.where(odd, right, left).astype(BF)
    for i, v in enumerate((up, above, below)):
        rows = slice(4 * GROUP + 8 * i, 4 * GROUP + 8 * i + 8)
        tile = v[PER_RT:, :].astype(BF)
        first_ref[rows, :] = tile
        second_ref[rows, :] = tile


def columns_of(tile):
    t = jnp.transpose(tile.astype(F32)[:, :384], (1, 0))
    return [t[(g % 4) * GROUP : (g % 4 + 1) * GROUP, g // 4 : g // 4 + 1] for g in range(8)]


def second_body(arrays, windows_of, g1_ref, g2_ref, hbm, weights, out_hbm, scratch, rts):
    o_s, x_s, y_s, out_sem, *sem = scratch
    wq, wp, wu, wd = weights
    arrived = (lambda *which: None) if hbm is None else Inputs(second_copies(hbm, weights), sem[0]).wait
    g1, g2 = g1_ref[1:2, :], g2_ref[1:2, :]
    windows, parts, inner = windows_of(*arrays), [], []
    for own, halo in windows:
        n_own = len(own) * GROUP
        x = jnp.concatenate([s[0].astype(F32) for s in own + halo], axis=0)
        lab = jnp.concatenate([s[1] for s in own + halo], axis=0)
        a = layer_norm(x, g1).astype(BF)
        kv = jnp.dot(a, wq[:, D:], preferred_element_type=F32).astype(BF)
        q = jnp.dot(a[:n_own], wq[:, :D], preferred_element_type=F32).astype(BF)
        inner.append(x[:n_own])
        parts.append((q, kv[:, :D], kv[:, D:], query_features(lab[:n_own], n_own), key_features(lab, 4 * GROUP)))
    for (own, _), x, o in zip(windows, inner, attend_all(parts)):
        for i, s in enumerate(own):
            at, side = s[2]
            for r in range(3):
                rows = piece(at * 3 + r, side)
                o_s[rows, :] = o[i * GROUP + r * PIECE : i * GROUP + (r + 1) * PIECE]
                x_s[rows, :] = x[i * GROUP + r * PIECE : i * GROUP + (r + 1) * PIECE]
    arrived(0)
    h = x_s[...] + jnp.dot(o_s[...].astype(BF), wp[...], preferred_element_type=F32)
    o_s[...] = mlp(h, g2, wu, wd, lambda *which: arrived(*[1 + w for w in which]))
    copies = []
    for i, rt in enumerate(rts):
        for n in range(36):
            t = i * PER_RT + n * LEV
            y_s[i * 3 + n // COLS, n % COLS] = o_s[t : t + LEV, :].astype(BF)
        c = pltpu.make_async_copy(y_s.at[i * 3 : i * 3 + 3], out_hbm.at[rt * 3 : rt * 3 + 3], out_sem.at[i])
        c.start()
        copies.append(c)
    for c in copies:
        c.wait()


def rows_of(ref, i):
    return ref[i * GROUP : (i + 1) * GROUP, :]


def middle_windows(own_one, own_two, one, two):
    left, right = both_ways("lon", own_one, own_two)
    left_halo, right_halo = both_ways("lon", one, two)
    mine = columns_of(left[PER_RT:, :])
    windows = []
    for side, (own_ref, halo_ref) in enumerate(((left, left_halo), (right, right_halo))):
        theirs = columns_of(halo_ref[PER_RT:, :])
        own = [(rows_of(own_ref, rt - 1), mine[rt * 2 + side], (rt - 1, side)) for rt in (1, 2)]
        halo = [(rows_of(halo_ref, rt - 1), theirs[rt * 2 + 1 - side]) for rt in (1, 2)]
        windows.append((own, halo))
    return windows


def edge_windows(own_one, own_two, v_one, v_two, h_one, h_two):
    up, down = both_ways("lat", own_one, own_two)
    above, below = both_ways("lat", v_one, v_two)
    left_halo, right_halo = both_ways("lon", h_one, h_two)
    mine = columns_of(up[PER_RT:, :])
    beside = []
    for ref in (left_halo, right_halo):
        beside.append([columns_of(ref[4 * GROUP + 8 * i : 4 * GROUP + 8 * i + 8, :]) for i in range(3)])
    windows = []
    for at, (rt, own_ref, v_ref) in enumerate(((0, up, above), (3, down, below))):
        theirs = columns_of(v_ref[PER_RT:, :])
        for side, ref in enumerate((left_halo, right_halo)):
            labels = beside[side]
            own = [(rows_of(own_ref, side), mine[rt * 2 + side], (at, side))]
            halo = [
                (rows_of(v_ref, side), theirs[(3 - rt) * 2 + side]),
                (rows_of(ref, at), labels[0][rt * 2 + 1 - side]),
                (rows_of(ref, 2 + at), labels[1 + at][(3 - rt) * 2 + 1 - side]),
            ]
            windows.append((own, halo))
    return windows


def second_copies(hbm, weights):
    wp_hbm, wu_hbm, wd_hbm = hbm
    wp, wu, wd = weights[1:]
    return [(wp_hbm.at[1], wp)] + mlp_chunks(wu_hbm, wd_hbm, 1, wu, wd)


def middle_kernel(a, b, c, d, g1_ref, g2_ref, wq, wp_hbm, wu_hbm, wd_hbm, out_hbm, wp, wu, wd, *scratch):
    hbm = (wp_hbm, wu_hbm, wd_hbm)
    second_body((a, b, c, d), middle_windows, g1_ref, g2_ref, hbm, (wq, wp, wu, wd), out_hbm, scratch, (1, 2))


def edge_kernel(out_in, a, b, c, d, e, f, g1_ref, g2_ref, wq, wp, wu, wd, out_hbm, *scratch):
    weights = (wq, wp, wu, wd)
    second_body((a, b, c, d, e, f), edge_windows, g1_ref, g2_ref, None, weights, out_hbm, scratch, (0, 3))


WEIGHT_SCRATCH = [pltpu.VMEM((D, 3 * D), BF), pltpu.VMEM((D, D), BF)]


def dma(n):
    return pltpu.SemaphoreType.DMA((n,))


SECOND_SCRATCH = [
    pltpu.VMEM((HALF, D), F32),
    pltpu.VMEM((HALF, D), F32),
    pltpu.VMEM((6, COLS, LEV, D), BF),
    dma(2),
]

VM = pl.BlockSpec(memory_space=pltpu.VMEM)
ANY = pl.BlockSpec(memory_space=pl.ANY)
HBM = pl.BlockSpec(memory_space=pltpu.HBM)


def cost(flops, nbytes):
    return pl.CostEstimate(flops=int(flops), bytes_accessed=int(nbytes), transcendentals=0)


def in_hbm(value):
    return pltpu.with_memory_space_constraint(value, pltpu.HBM)


def exchange(one, two, axis):
    count = lax.axis_size(axis)
    even_pairs = [(s, s + 1 - 2 * (s % 2)) for s in range(count)]
    odd_pairs = [(s, (s - 1 + 2 * (s % 2)) % count) for s in range(count)]
    return lax.ppermute(one, axis, even_pairs), lax.ppermute(two, axis, odd_pairs)


def first_calls(tokens, region, g1, g2, weights):
    pick, lane, adds = token_tables()
    tables = [in_hbm(jnp.asarray(t, d)) for t, d in ((pick, BF), (lane, BF), (adds, F32))]
    params = pltpu.CompilerParams(vmem_limit_bytes=VMEM_LIMIT)
    edge_out = jax.ShapeDtypeStruct((PER_RT + 8, D), BF)
    up, down, tile, mid, wu, g1, g2 = pl.pallas_call(
        first_kernel,
        out_shape=(
            edge_out, edge_out, pltpu.VMEM((8, D), BF), pltpu.VMEM((HALF, D), F32),
            pltpu.VMEM((D, FF), BF), pltpu.VMEM((2, D), F32), pltpu.VMEM((2, D), F32),
        ),
        in_specs=[HBM] * 11,
        out_specs=[VM] * 7,
        scratch_shapes=[
            pltpu.VMEM((ROWS, COLS, LEV, D), BF), pltpu.VMEM((D // 128, TOKENS, 128), F32), pltpu.VMEM((HALF, 128), F32),
            pltpu.VMEM((384, 128), F32), pltpu.VMEM((ROWS, LEV, COLS), jnp.int32), pltpu.VMEM((HALF, 128), BF),
            pltpu.VMEM((HALF, 128), BF), pltpu.VMEM((HALF, 128), F32),
        ] + WEIGHT_SCRATCH + [pltpu.VMEM((FF, D), BF), dma(4), dma(N_CHUNK), dma(6)],
        compiler_params=params,
        cost_estimate=cost(4e9, 8e6),
        name="first_block",
    )(tokens, region, *tables, g1, g2, *weights)
    left, right, early = pl.pallas_call(
        middle_mlp_kernel,
        out_shape=(edge_out, edge_out, pltpu.VMEM((D, 3 * D), BF)),
        in_specs=[VM] * 4 + [HBM] * 2,
        out_specs=[VM] * 3,
        scratch_shapes=[pltpu.VMEM((FF, D), BF), dma(N_CHUNK // 2 + 1)],
        compiler_params=params,
        cost_estimate=cost(1.3e9, 5e6),
        name="first_middle",
    )(mid, tile, g2, wu, weights[3], weights[0])
    return up, down, left, right, g1, g2, early


def second_calls(middle, edge, g1, g2, early, weights):
    params = pltpu.CompilerParams(vmem_limit_bytes=VMEM_LIMIT)
    out_shape = jax.ShapeDtypeStruct((ROWS, COLS, LEV, D), BF)
    out, *late = pl.pallas_call(
        middle_kernel,
        out_shape=(
            out_shape, pltpu.VMEM((D, D), BF), pltpu.VMEM((D, FF), BF), pltpu.VMEM((FF, D), BF),
        ),
        in_specs=[VM] * 7 + [HBM] * 3,
        out_specs=[HBM] + [VM] * 3,
        scratch_shapes=SECOND_SCRATCH + [dma(1 + N_CHUNK)],
        compiler_params=params,
        cost_estimate=cost(2.5e9, 8e6),
        name="second_middle",
    )(*middle, g1, g2, early, *weights[1:])
    return pl.pallas_call(
        edge_kernel,
        out_shape=out_shape,
        in_specs=[HBM] + [VM] * 12,
        out_specs=HBM,
        scratch_shapes=SECOND_SCRATCH,
        input_output_aliases={0: 0},
        compiler_params=params,
        cost_estimate=cost(2.5e9, 8e6),
        name="second_edge",
    )(out, *edge, g1, g2, early, *late)


def per_device(tokens, region, norm_gain1, qkv_weight, proj_weight, norm_gain2, up_weight, down_weight):
    weights = [in_hbm(w) for w in (qkv_weight, proj_weight, up_weight, down_weight)]
    g1, g2 = in_hbm(norm_gain1), in_hbm(norm_gain2)
    up, down, left, right, g1, g2, early = first_calls(
        in_hbm(jnp.transpose(tokens, (1, 2, 0, 3))), in_hbm(jnp.transpose(region, (1, 0, 2))), g1, g2, weights
    )
    received = exchange(up, down, "lat")
    above, below = received
    left, right, above = lax.optimization_barrier((left, right, above))
    halo = exchange(left, right, "lon")
    message = jax.ShapeDtypeStruct((4 * GROUP + 24, D), BF)
    packed = pl.pallas_call(
        pack_kernel,
        out_shape=(message, message),
        in_specs=[VM] * 4,
        out_specs=[VM] * 2,
        compiler_params=pltpu.CompilerParams(vmem_limit_bytes=8 * 1024 * 1024),
        cost_estimate=cost(1e6, 1e6),
        name="pack_edges",
    )(up, down, above, below)
    beside = exchange(*packed, "lon")
    out = second_calls((left, right, *halo), (up, down, above, below, *beside), g1, g2, early, weights)
    return jnp.transpose(out, (2, 0, 1, 3))


def solution(mesh):
    return jax.shard_map(
        per_device,
        mesh=mesh,
        in_specs=(P(None, "lat", "lon", None), P(None, "lat", "lon"), P(), P(), P(), P(), P(), P()),
        out_specs=P(None, "lat", "lon", None),
        check_vma=False,
    )
```

```python
import math

import jax
import jax.numpy as jnp
import numpy as np
from jax import lax
from jax.experimental import pallas as pl
from jax.experimental.pallas import tpu as pltpu
from jax.sharding import PartitionSpec as P

BF = jnp.bfloat16
F32 = jnp.float32
LEV, D, FF, HEADS, HD = 4, 512, 2048, 8, 64
ROWS = COLS = 12
PIECE = 6 * LEV
GROUP = 3 * PIECE
PER_RT = 2 * GROUP
HALF = 2 * PER_RT
TOKENS = 2 * HALF
EPS = 1e-05
BIG = 1e30
EXP_SCALE = math.log2(math.e) / math.sqrt(HD)
VMEM_LIMIT = 24 * 1024 * 1024
FCHUNK = 1024
PER_LEVEL = HALF // LEV


def token_tables():
    pick = np.zeros((HALF, 128), np.float32)
    lane = np.zeros((HALF, 128), np.float32)
    for row in range(6):
        for col in range(COLS):
            for level in range(LEV):
                t = (row * COLS + col) * LEV + level
                pick[t, row * LEV + level] = 1.0
                lane[t, col] = 1.0
    level = np.arange(HALF) % LEV
    row = np.arange(HALF) // (COLS * LEV)
    adds = np.zeros((HALF, 128), np.float32)
    adds[:, 1] = 4 * (level == 0) + np.where((level == 1) | (level == 2), 0, 1)
    adds[:, 2] = 2 * (row < 3)
    return pick, lane, adds


def layer_norm(x, gain):
    mean = jnp.mean(x, axis=-1, keepdims=True)
    centered = x - mean
    variance = jnp.mean(centered * centered, axis=-1, keepdims=True)
    return centered * lax.rsqrt(variance + EPS) * gain


def one_hot(labels, rows):
    lane = lax.broadcasted_iota(jnp.int32, (rows, 128), 1) & 63
    return lane.astype(F32) == labels


def query_features(labels, rows):
    return jnp.where(one_hot(labels, rows), -BIG, 0.0).astype(BF)


def key_features(labels, rows):
    return jnp.where(one_hot(labels, rows), 0.0, 1.0).astype(BF)


def low_lanes(rows):
    return lax.broadcasted_iota(jnp.int32, (rows, 128), 1) < 64


def attend_all(parts):
    jobs = [(part, h) for part in parts for h in range(HEADS)]
    scores, weights, got = [], [], []
    for (q, k, v, qf, kf), h in jobs:
        lanes = slice(h // 2 * 128, (h // 2 + 1) * 128)
        low_q, low_k = low_lanes(q.shape[0]), low_lanes(k.shape[0])
        if h % 2:
            qh, kh = jnp.where(low_q, qf, q[:, lanes]), jnp.where(low_k, kf, k[:, lanes])
        else:
            qh, kh = jnp.where(low_q, q[:, lanes], qf), jnp.where(low_k, k[:, lanes], kf)
        scores.append(lax.dot_general(qh, kh, (((1,), (1,)), ((), ())), preferred_element_type=F32))
    for s in scores:
        peak = jnp.max(s, axis=-1, keepdims=True)
        weights.append(jnp.exp2((s - peak) * EXP_SCALE).astype(BF))
    for ((q, k, v, qf, kf), h), e in zip(jobs, weights):
        lanes = slice(h // 2 * 128, (h // 2 + 1) * 128)
        low_k, ones = low_lanes(k.shape[0]), jnp.ones((k.shape[0], 128), BF)
        vh = jnp.where(low_k, ones, v[:, lanes]) if h % 2 else jnp.where(low_k, v[:, lanes], ones)
        got.append(jnp.dot(e, vh, preferred_element_type=F32))
    outs = []
    for i, part in enumerate(parts):
        low_q = low_lanes(part[0].shape[0])
        tiles = []
        for even, odd in zip(got[i * HEADS : (i + 1) * HEADS : 2], got[i * HEADS + 1 : (i + 1) * HEADS : 2]):
            num = jnp.where(low_q, even, odd)
            den = pltpu.roll(jnp.where(low_q, odd, even), 64, 1)
            tiles.append(num / den)
        outs.append(jnp.concatenate(tiles, axis=1))
    return outs


def attend(*part):
    return attend_all([part])[0]


def is_odd(axis):
    return lax.rem(lax.axis_index(axis), 2) == 1


def token_labels(region_ref, half, pick_ref, lane_ref, adds_ref, lab_s, first_row):
    lab_s[0:128, :] = jnp.zeros((128, 128), F32)
    for row in range(6):
        lab_s[row * LEV : (row + 1) * LEV, 0:COLS] = region_ref[half * 6 + row].astype(F32)
    rows = jnp.dot(pick_ref[...], lab_s[0:128, :].astype(BF), preferred_element_type=F32)
    region = jnp.sum(rows * lane_ref[...].astype(F32), axis=-1, keepdims=True)
    lab2 = region * 8 + adds_ref[:, 1:2]
    if half == 0:
        lab2 = lab2 + adds_ref[:, 2:3] * first_row
    lab_s[...] = jnp.broadcast_to(region, (HALF, 128))
    lab1 = jnp.concatenate([lab_s[pl.ds(level, PER_LEVEL, stride=LEV), :] for level in range(LEV)], axis=0)[:, 0:1]
    return lab1, lab2


def load_rows(ref, rows):
    return jnp.concatenate([ref[j, rows, :] for j in range(D // 128)], axis=1)


def store_rows(ref, rows, value):
    for j in range(D // 128):
        ref[j, rows, :] = value[:, j * 128 : (j + 1) * 128]


def piece(row, side):
    start = row * 2 * PIECE + side * PIECE
    return slice(start, start + PIECE)


def grouped(value, rt, side):
    return jnp.concatenate([value[piece(rt * 3 + r, side)] for r in range(3)], axis=0)


class Inputs:
    def __init__(self, pairs, sem):
        self.copies = [pltpu.make_async_copy(s, b, sem.at[i]) for i, (s, b) in enumerate(pairs)]
        for c in self.copies:
            c.start()

    def wait(self, *which):
        for i in which:
            self.copies[i].wait()


def mlp_chunks(wu_hbm, wd_hbm, block, wu, wd):
    pairs = []
    for c in range(0, FF, FCHUNK):
        pairs.append((wu_hbm.at[block, :, c : c + FCHUNK], wu.at[:, c : c + FCHUNK]))
        pairs.append((wd_hbm.at[block, c : c + FCHUNK, :], wd.at[c : c + FCHUNK, :]))
    return pairs


N_CHUNK = 2 * (FF // FCHUNK)


def mlp(h, gain, wup, wdown, arrived, chunk=FCHUNK):
    a = layer_norm(h, gain).astype(BF)
    acc = h
    for c in range(0, FF, chunk):
        arrived(*range(2 * (c // FCHUNK), 2 * ((c + chunk) // FCHUNK)))
        u = jnp.dot(a, wup[:, c : c + chunk], preferred_element_type=F32)
        g = jax.nn.gelu(u).astype(BF)
        acc = acc + jnp.dot(g, wdown[c : c + chunk, :], preferred_element_type=F32)
    return acc


def first_kernel(
    x_hbm, region_hbm, pick_hbm, lane_hbm, adds_hbm, g1_hbm, g2_hbm, wq_hbm, wp_hbm, wu_hbm, wd_hbm,
    one_ref, two_ref, tile_ref, mid_ref, wu, g1_ref, g2_ref,
    xv, xs, lab_s, labs, region_ref, pick_ref, lane_ref, adds_ref, wq, wp, wd, sem, mlp_sem, small_sem,
):
    small = Inputs(
        [
            (region_hbm, region_ref), (pick_hbm, pick_ref), (lane_hbm, lane_ref), (adds_hbm, adds_ref),
            (g1_hbm, g1_ref), (g2_hbm, g2_ref),
        ],
        small_sem,
    )
    inputs = Inputs(
        [(x_hbm.at[0:6], xv.at[0:6]), (wq_hbm.at[0], wq), (x_hbm.at[6:12], xv.at[6:12]), (wp_hbm.at[0], wp)], sem
    )
    first_row = (lax.axis_index("lat") == 0).astype(F32)
    small.wait(*range(6))
    g1, g2 = g1_ref[0:1, :], g2_ref[0:1, :]
    tiles, features, strides = [], [], []
    for half in range(2):
        lab1, lab2 = token_labels(region_ref, half, pick_ref, lane_ref, adds_ref, lab_s, first_row)
        features += [(query_features(lab1[p], 144), key_features(lab1[p], 144)) for p in (slice(0, 144), slice(144, 288))]
        for i in range(2):
            for side in range(2):
                start = (i * 2 + side) * GROUP
                labs[start : start + GROUP, :] = jnp.broadcast_to(grouped(lab2, i, side), (GROUP, 128))
        tiles.append(jnp.transpose(labs[...], (1, 0))[0:8])
    for half in range(2):
        inputs.wait(2 * half)
        for n in range(half * 72, half * 72 + 72):
            store_rows(xs, slice(n * LEV, (n + 1) * LEV), xv[n // COLS, n % COLS].astype(F32))
        strides += [pl.ds(half * HALF + level, PER_LEVEL, stride=LEV) for level in range(LEV)]
    x = jnp.concatenate([load_rows(xs, rows) for rows in strides], axis=0)
    a = layer_norm(x, g1).astype(BF)
    inputs.wait(1)
    mlp_inputs = Inputs(mlp_chunks(wu_hbm, wd_hbm, 0, wu, wd), mlp_sem)
    qkv = jnp.dot(a, wq[...], preferred_element_type=F32).astype(BF)
    parts = []
    for i, (qf, kf) in enumerate(features):
        p = slice(i * 144, (i + 1) * 144)
        parts.append((qkv[p, :D], qkv[p, D : 2 * D], qkv[p, 2 * D :], qf, kf))
    o = jnp.concatenate(attend_all(parts), axis=0).astype(BF)
    inputs.wait(3)
    h = x + jnp.dot(o, wp[...], preferred_element_type=F32)
    for i, rows in enumerate(strides):
        store_rows(xs, rows, h[i * PER_LEVEL : (i + 1) * PER_LEVEL])
    mid_ref[...] = load_rows(xs, slice(PER_RT, 3 * PER_RT))
    row = lax.broadcasted_iota(jnp.int32, (8, 384), 0)
    tile = jnp.where(row == 0, tiles[0], tiles[1])
    tile = jnp.concatenate([tile, jnp.zeros((8, 128), F32)], axis=1).astype(BF)
    tile_ref[...] = tile
    h = jnp.concatenate([load_rows(xs, slice(0, PER_RT)), load_rows(xs, slice(3 * PER_RT, TOKENS))], axis=0)
    y = mlp(h, g2, wu, wd, mlp_inputs.wait, FF)
    odd = is_odd("lat")
    for side in range(2):
        rows = slice(side * GROUP, (side + 1) * GROUP)
        up, down = grouped(y, 0, side), grouped(y, 1, side)
        one_ref[rows, :] = jnp.where(odd, up, down).astype(BF)
        two_ref[rows, :] = jnp.where(odd, down, up).astype(BF)
    one_ref[PER_RT:, :] = tile
    two_ref[PER_RT:, :] = tile


def middle_mlp_kernel(mid, tile_ref, g2_ref, wu, wd_hbm, wq_hbm, one_ref, two_ref, wq1, wd, sem):
    chunks = [slice(c, c + FCHUNK) for c in range(0, FF, FCHUNK)]
    inputs = Inputs([(wd_hbm.at[0, c], wd.at[c]) for c in chunks] + [(wq_hbm.at[1], wq1)], sem)
    y = mlp(mid[...], g2_ref[0:1, :], wu, wd, lambda up, down: inputs.wait(down // 2))
    odd = is_odd("lon")
    for i in range(2):
        rows = slice(i * GROUP, (i + 1) * GROUP)
        left, right = grouped(y, i, 0), grouped(y, i, 1)
        one_ref[rows, :] = jnp.where(odd, left, right).astype(BF)
        two_ref[rows, :] = jnp.where(odd, right, left).astype(BF)
    one_ref[PER_RT:, :] = tile_ref[...]
    two_ref[PER_RT:, :] = tile_ref[...]
    inputs.wait(N_CHUNK // 2)


class Either:
    def __init__(self, odd, first, second):
        self.odd, self.first, self.second = odd, first, second

    def __getitem__(self, at):
        return jnp.where(self.odd, self.first[at].astype(F32), self.second[at].astype(F32))


def both_ways(axis, one, two):
    odd = is_odd(axis)
    return Either(odd, one, two), Either(odd, two, one)


def pack_kernel(own_one, own_two, one, two, first_ref, second_ref):
    up, down = both_ways("lat", own_one, own_two)
    above, below = both_ways("lat", one, two)
    odd = is_odd("lon")
    for i, v in enumerate((up, down, above, below)):
        left, right = (v[side * GROUP : (side + 1) * GROUP, :] for side in range(2))
        rows = slice(i * GROUP, (i + 1) * GROUP)
        first_ref[rows, :] = jnp.where(odd, left, right).astype(BF)
        second_ref[rows, :] = jnp.where(odd, right, left).astype(BF)
    for i, v in enumerate((up, above, below)):
        rows = slice(4 * GROUP + 8 * i, 4 * GROUP + 8 * i + 8)
        tile = v[PER_RT:, :].astype(BF)
        first_ref[rows, :] = tile
        second_ref[rows, :] = tile


def columns_of(tile):
    t = jnp.transpose(tile.astype(F32)[:, :384], (1, 0))
    return [t[(g % 4) * GROUP : (g % 4 + 1) * GROUP, g // 4 : g // 4 + 1] for g in range(8)]


def second_body(arrays, windows_of, g1_ref, g2_ref, hbm, weights, out_hbm, scratch, rts):
    o_s, x_s, y_s, out_sem, *sem = scratch
    wq, wp, wu, wd = weights
    arrived = (lambda *which: None) if hbm is None else Inputs(second_copies(hbm, weights), sem[0]).wait
    g1, g2 = g1_ref[1:2, :], g2_ref[1:2, :]
    windows, parts, inner = windows_of(*arrays), [], []
    for own, halo in windows:
        n_own = len(own) * GROUP
        x = jnp.concatenate([s[0].astype(F32) for s in own + halo], axis=0)
        lab = jnp.concatenate([s[1] for s in own + halo], axis=0)
        a = layer_norm(x, g1).astype(BF)
        kv = jnp.dot(a, wq[:, D:], preferred_element_type=F32).astype(BF)
        q = jnp.dot(a[:n_own], wq[:, :D], preferred_element_type=F32).astype(BF)
        inner.append(x[:n_own])
        parts.append((q, kv[:, :D], kv[:, D:], query_features(lab[:n_own], n_own), key_features(lab, 4 * GROUP)))
    for (own, _), x, o in zip(windows, inner, attend_all(parts)):
        for i, s in enumerate(own):
            at, side = s[2]
            for r in range(3):
                rows = piece(at * 3 + r, side)
                o_s[rows, :] = o[i * GROUP + r * PIECE : i * GROUP + (r + 1) * PIECE]
                x_s[rows, :] = x[i * GROUP + r * PIECE : i * GROUP + (r + 1) * PIECE]
    arrived(0)
    h = x_s[...] + jnp.dot(o_s[...].astype(BF), wp[...], preferred_element_type=F32)
    o_s[...] = mlp(h, g2, wu, wd, lambda *which: arrived(*[1 + w for w in which]), FF if hbm is None else FCHUNK)
    copies = []
    for i, rt in enumerate(rts):
        for n in range(36):
            t = i * PER_RT + n * LEV
            y_s[i * 3 + n // COLS, n % COLS] = o_s[t : t + LEV, :].astype(BF)
        c = pltpu.make_async_copy(y_s.at[i * 3 : i * 3 + 3], out_hbm.at[rt * 3 : rt * 3 + 3], out_sem.at[i])
        c.start()
        copies.append(c)
    for c in copies:
        c.wait()


def rows_of(ref, i):
    return ref[i * GROUP : (i + 1) * GROUP, :]


def middle_windows(own_one, own_two, one, two):
    left, right = both_ways("lon", own_one, own_two)
    left_halo, right_halo = both_ways("lon", one, two)
    mine = columns_of(left[PER_RT:, :])
    windows = []
    for side, (own_ref, halo_ref) in enumerate(((left, left_halo), (right, right_halo))):
        theirs = columns_of(halo_ref[PER_RT:, :])
        own = [(rows_of(own_ref, rt - 1), mine[rt * 2 + side], (rt - 1, side)) for rt in (1, 2)]
        halo = [(rows_of(halo_ref, rt - 1), theirs[rt * 2 + 1 - side]) for rt in (1, 2)]
        windows.append((own, halo))
    return windows


def edge_windows(own_one, own_two, v_one, v_two, h_one, h_two):
    up, down = both_ways("lat", own_one, own_two)
    above, below = both_ways("lat", v_one, v_two)
    left_halo, right_halo = both_ways("lon", h_one, h_two)
    mine = columns_of(up[PER_RT:, :])
    beside = []
    for ref in (left_halo, right_halo):
        beside.append([columns_of(ref[4 * GROUP + 8 * i : 4 * GROUP + 8 * i + 8, :]) for i in range(3)])
    windows = []
    for at, (rt, own_ref, v_ref) in enumerate(((0, up, above), (3, down, below))):
        theirs = columns_of(v_ref[PER_RT:, :])
        for side, ref in enumerate((left_halo, right_halo)):
            labels = beside[side]
            own = [(rows_of(own_ref, side), mine[rt * 2 + side], (at, side))]
            halo = [
                (rows_of(v_ref, side), theirs[(3 - rt) * 2 + side]),
                (rows_of(ref, at), labels[0][rt * 2 + 1 - side]),
                (rows_of(ref, 2 + at), labels[1 + at][(3 - rt) * 2 + 1 - side]),
            ]
            windows.append((own, halo))
    return windows


def second_copies(hbm, weights):
    wp_hbm, wu_hbm, wd_hbm = hbm
    wp, wu, wd = weights[1:]
    return [(wp_hbm.at[1], wp)] + mlp_chunks(wu_hbm, wd_hbm, 1, wu, wd)


def middle_kernel(a, b, c, d, g1_ref, g2_ref, wq, wp_hbm, wu_hbm, wd_hbm, out_hbm, wp, wu, wd, *scratch):
    hbm = (wp_hbm, wu_hbm, wd_hbm)
    second_body((a, b, c, d), middle_windows, g1_ref, g2_ref, hbm, (wq, wp, wu, wd), out_hbm, scratch, (1, 2))


def edge_kernel(out_in, a, b, c, d, e, f, g1_ref, g2_ref, wq, wp, wu, wd, out_hbm, *scratch):
    weights = (wq, wp, wu, wd)
    second_body((a, b, c, d, e, f), edge_windows, g1_ref, g2_ref, None, weights, out_hbm, scratch, (0, 3))


WEIGHT_SCRATCH = [pltpu.VMEM((D, 3 * D), BF), pltpu.VMEM((D, D), BF)]


def dma(n):
    return pltpu.SemaphoreType.DMA((n,))


SECOND_SCRATCH = [
    pltpu.VMEM((HALF, D), F32),
    pltpu.VMEM((HALF, D), F32),
    pltpu.VMEM((6, COLS, LEV, D), BF),
    dma(2),
]

VM = pl.BlockSpec(memory_space=pltpu.VMEM)
ANY = pl.BlockSpec(memory_space=pl.ANY)
HBM = pl.BlockSpec(memory_space=pltpu.HBM)


def cost(flops, nbytes):
    return pl.CostEstimate(flops=int(flops), bytes_accessed=int(nbytes), transcendentals=0)


def in_hbm(value):
    return pltpu.with_memory_space_constraint(value, pltpu.HBM)


def exchange(one, two, axis):
    count = lax.axis_size(axis)
    even_pairs = [(s, s + 1 - 2 * (s % 2)) for s in range(count)]
    odd_pairs = [(s, (s - 1 + 2 * (s % 2)) % count) for s in range(count)]
    return lax.ppermute(one, axis, even_pairs), lax.ppermute(two, axis, odd_pairs)


def first_calls(tokens, region, g1, g2, weights):
    pick, lane, adds = token_tables()
    tables = [in_hbm(jnp.asarray(t, d)) for t, d in ((pick, BF), (lane, BF), (adds, F32))]
    params = pltpu.CompilerParams(vmem_limit_bytes=VMEM_LIMIT)
    edge_out = jax.ShapeDtypeStruct((PER_RT + 8, D), BF)
    up, down, tile, mid, wu, g1, g2 = pl.pallas_call(
        first_kernel,
        out_shape=(
            edge_out, edge_out, pltpu.VMEM((8, D), BF), pltpu.VMEM((HALF, D), F32),
            pltpu.VMEM((D, FF), BF), pltpu.VMEM((2, D), F32), pltpu.VMEM((2, D), F32),
        ),
        in_specs=[HBM] * 11,
        out_specs=[VM] * 7,
        scratch_shapes=[
            pltpu.VMEM((ROWS, COLS, LEV, D), BF), pltpu.VMEM((D // 128, TOKENS, 128), F32), pltpu.VMEM((HALF, 128), F32),
            pltpu.VMEM((384, 128), F32), pltpu.VMEM((ROWS, LEV, COLS), jnp.int32), pltpu.VMEM((HALF, 128), BF),
            pltpu.VMEM((HALF, 128), BF), pltpu.VMEM((HALF, 128), F32),
        ] + WEIGHT_SCRATCH + [pltpu.VMEM((FF, D), BF), dma(4), dma(N_CHUNK), dma(6)],
        compiler_params=params,
        cost_estimate=cost(4e9, 8e6),
        name="first_block",
    )(tokens, region, *tables, g1, g2, *weights)
    left, right, early = pl.pallas_call(
        middle_mlp_kernel,
        out_shape=(edge_out, edge_out, pltpu.VMEM((D, 3 * D), BF)),
        in_specs=[VM] * 4 + [HBM] * 2,
        out_specs=[VM] * 3,
        scratch_shapes=[pltpu.VMEM((FF, D), BF), dma(N_CHUNK // 2 + 1)],
        compiler_params=params,
        cost_estimate=cost(1.3e9, 5e6),
        name="first_middle",
    )(mid, tile, g2, wu, weights[3], weights[0])
    return up, down, left, right, g1, g2, early


def second_calls(middle, edge, g1, g2, early, weights):
    params = pltpu.CompilerParams(vmem_limit_bytes=VMEM_LIMIT)
    out_shape = jax.ShapeDtypeStruct((ROWS, COLS, LEV, D), BF)
    out, *late = pl.pallas_call(
        middle_kernel,
        out_shape=(
            out_shape, pltpu.VMEM((D, D), BF), pltpu.VMEM((D, FF), BF), pltpu.VMEM((FF, D), BF),
        ),
        in_specs=[VM] * 7 + [HBM] * 3,
        out_specs=[HBM] + [VM] * 3,
        scratch_shapes=SECOND_SCRATCH + [dma(1 + N_CHUNK)],
        compiler_params=params,
        cost_estimate=cost(2.5e9, 8e6),
        name="second_middle",
    )(*middle, g1, g2, early, *weights[1:])
    return pl.pallas_call(
        edge_kernel,
        out_shape=out_shape,
        in_specs=[HBM] + [VM] * 12,
        out_specs=HBM,
        scratch_shapes=SECOND_SCRATCH,
        input_output_aliases={0: 0},
        compiler_params=params,
        cost_estimate=cost(2.5e9, 8e6),
        name="second_edge",
    )(out, *edge, g1, g2, early, *late)


def per_device(tokens, region, norm_gain1, qkv_weight, proj_weight, norm_gain2, up_weight, down_weight):
    weights = [in_hbm(w) for w in (qkv_weight, proj_weight, up_weight, down_weight)]
    g1, g2 = in_hbm(norm_gain1), in_hbm(norm_gain2)
    up, down, left, right, g1, g2, early = first_calls(
        in_hbm(jnp.transpose(tokens, (1, 2, 0, 3))), in_hbm(jnp.transpose(region, (1, 0, 2))), g1, g2, weights
    )
    received = exchange(up, down, "lat")
    above, below = received
    left, right, above = lax.optimization_barrier((left, right, above))
    halo = exchange(left, right, "lon")
    message = jax.ShapeDtypeStruct((4 * GROUP + 24, D), BF)
    packed = pl.pallas_call(
        pack_kernel,
        out_shape=(message, message),
        in_specs=[VM] * 4,
        out_specs=[VM] * 2,
        compiler_params=pltpu.CompilerParams(vmem_limit_bytes=8 * 1024 * 1024),
        cost_estimate=cost(1e6, 1e6),
        name="pack_edges",
    )(up, down, above, below)
    beside = exchange(*packed, "lon")
    out = second_calls((left, right, *halo), (up, down, above, below, *beside), g1, g2, early, weights)
    return jnp.transpose(out, (2, 0, 1, 3))


def solution(mesh):
    return jax.shard_map(
        per_device,
        mesh=mesh,
        in_specs=(P(None, "lat", "lon", None), P(None, "lat", "lon"), P(), P(), P(), P(), P(), P()),
        out_specs=P(None, "lat", "lon", None),
        check_vma=False,
    )
```

```python
import math

import jax
import jax.numpy as jnp
import numpy as np
from jax import lax
from jax.experimental import pallas as pl
from jax.experimental.pallas import tpu as pltpu
from jax.sharding import PartitionSpec as P

BF = jnp.bfloat16
F32 = jnp.float32
LEV, D, FF, HEADS, HD = 4, 512, 2048, 8, 64
ROWS = COLS = 12
PIECE = 6 * LEV
GROUP = 3 * PIECE
PER_RT = 2 * GROUP
HALF = 2 * PER_RT
TOKENS = 2 * HALF
EPS = 1e-05
BIG = 1e30
EXP_SCALE = math.log2(math.e) / math.sqrt(HD)
VMEM_LIMIT = 24 * 1024 * 1024
FCHUNK = 1024
PER_LEVEL = HALF // LEV


def token_tables():
    pick = np.zeros((HALF, 128), np.float32)
    lane = np.zeros((HALF, 128), np.float32)
    for row in range(6):
        for col in range(COLS):
            for level in range(LEV):
                t = (row * COLS + col) * LEV + level
                pick[t, row * LEV + level] = 1.0
                lane[t, col] = 1.0
    level = np.arange(HALF) % LEV
    row = np.arange(HALF) // (COLS * LEV)
    adds = np.zeros((HALF, 128), np.float32)
    adds[:, 1] = 4 * (level == 0) + np.where((level == 1) | (level == 2), 0, 1)
    adds[:, 2] = 2 * (row < 3)
    return pick, lane, adds


def layer_norm(x, gain):
    mean = jnp.mean(x, axis=-1, keepdims=True)
    centered = x - mean
    variance = jnp.mean(centered * centered, axis=-1, keepdims=True)
    return centered * lax.rsqrt(variance + EPS) * gain


def one_hot(labels, rows):
    lane = lax.broadcasted_iota(jnp.int32, (rows, 128), 1) & 63
    return lane.astype(F32) == labels


def query_features(labels, rows):
    return jnp.where(one_hot(labels, rows), -BIG, 0.0).astype(BF)


def key_features(labels, rows):
    return jnp.where(one_hot(labels, rows), 0.0, 1.0).astype(BF)


def low_lanes(rows):
    return lax.broadcasted_iota(jnp.int32, (rows, 128), 1) < 64


def attend_all(parts):
    jobs = [(part, h) for part in parts for h in range(HEADS)]
    scores, weights, got = [], [], []
    for (q, k, v, qf, kf), h in jobs:
        lanes = slice(h // 2 * 128, (h // 2 + 1) * 128)
        low_q, low_k = low_lanes(q.shape[0]), low_lanes(k.shape[0])
        if h % 2:
            qh, kh = jnp.where(low_q, qf, q[:, lanes]), jnp.where(low_k, kf, k[:, lanes])
        else:
            qh, kh = jnp.where(low_q, q[:, lanes], qf), jnp.where(low_k, k[:, lanes], kf)
        scores.append(lax.dot_general(qh, kh, (((1,), (1,)), ((), ())), preferred_element_type=F32))
    for s in scores:
        peak = jnp.max(s, axis=-1, keepdims=True)
        weights.append(jnp.exp2((s - peak) * EXP_SCALE).astype(BF))
    for ((q, k, v, qf, kf), h), e in zip(jobs, weights):
        lanes = slice(h // 2 * 128, (h // 2 + 1) * 128)
        low_k, ones = low_lanes(k.shape[0]), jnp.ones((k.shape[0], 128), BF)
        vh = jnp.where(low_k, ones, v[:, lanes]) if h % 2 else jnp.where(low_k, v[:, lanes], ones)
        got.append(jnp.dot(e, vh, preferred_element_type=F32))
    outs = []
    for i, part in enumerate(parts):
        low_q = low_lanes(part[0].shape[0])
        tiles = []
        for even, odd in zip(got[i * HEADS : (i + 1) * HEADS : 2], got[i * HEADS + 1 : (i + 1) * HEADS : 2]):
            num = jnp.where(low_q, even, odd)
            den = pltpu.roll(jnp.where(low_q, odd, even), 64, 1)
            tiles.append(num / den)
        outs.append(jnp.concatenate(tiles, axis=1))
    return outs


def attend(*part):
    return attend_all([part])[0]


def is_odd(axis):
    return lax.rem(lax.axis_index(axis), 2) == 1


def token_labels(region_ref, half, pick_ref, lane_ref, adds_ref, lab_s, first_row):
    lab_s[0:128, :] = jnp.zeros((128, 128), F32)
    for row in range(6):
        lab_s[row * LEV : (row + 1) * LEV, 0:COLS] = region_ref[half * 6 + row].astype(F32)
    rows = jnp.dot(pick_ref[...], lab_s[0:128, :].astype(BF), preferred_element_type=F32)
    region = jnp.sum(rows * lane_ref[...].astype(F32), axis=-1, keepdims=True)
    lab2 = region * 8 + adds_ref[:, 1:2]
    if half == 0:
        lab2 = lab2 + adds_ref[:, 2:3] * first_row
    lab_s[...] = jnp.broadcast_to(region, (HALF, 128))
    lab1 = jnp.concatenate([lab_s[pl.ds(level, PER_LEVEL, stride=LEV), :] for level in range(LEV)], axis=0)[:, 0:1]
    return lab1, lab2


def load_rows(ref, rows):
    return jnp.concatenate([ref[j, rows, :] for j in range(D // 128)], axis=1)


def store_rows(ref, rows, value):
    for j in range(D // 128):
        ref[j, rows, :] = value[:, j * 128 : (j + 1) * 128]


def piece(row, side):
    start = row * 2 * PIECE + side * PIECE
    return slice(start, start + PIECE)


def grouped(value, rt, side):
    return jnp.concatenate([value[piece(rt * 3 + r, side)] for r in range(3)], axis=0)


class Inputs:
    def __init__(self, pairs, sem):
        self.copies = [pltpu.make_async_copy(s, b, sem.at[i]) for i, (s, b) in enumerate(pairs)]
        for c in self.copies:
            c.start()

    def wait(self, *which):
        for i in which:
            self.copies[i].wait()


def mlp_chunks(wu_hbm, wd_hbm, block, wu, wd):
    pairs = []
    for c in range(0, FF, FCHUNK):
        pairs.append((wu_hbm.at[block, :, c : c + FCHUNK], wu.at[:, c : c + FCHUNK]))
        pairs.append((wd_hbm.at[block, c : c + FCHUNK, :], wd.at[c : c + FCHUNK, :]))
    return pairs


N_CHUNK = 2 * (FF // FCHUNK)


def mlp(h, gain, wup, wdown, arrived, chunk=FCHUNK):
    a = layer_norm(h, gain).astype(BF)
    acc = h
    for c in range(0, FF, chunk):
        arrived(*range(2 * (c // FCHUNK), 2 * ((c + chunk) // FCHUNK)))
        u = jnp.dot(a, wup[:, c : c + chunk], preferred_element_type=F32)
        g = jax.nn.gelu(u).astype(BF)
        acc = acc + jnp.dot(g, wdown[c : c + chunk, :], preferred_element_type=F32)
    return acc


def first_kernel(
    x_hbm, region_hbm, pick_hbm, lane_hbm, adds_hbm, g1_hbm, g2_hbm, wq_hbm, wp_hbm, wu_hbm, wd_hbm,
    one_ref, two_ref, tile_ref, mid_ref, wu, g1_ref, g2_ref,
    xv, xs, lab_s, labs, region_ref, pick_ref, lane_ref, adds_ref, wq, wp, wd, sem, mlp_sem, small_sem,
):
    inputs = Inputs(
        [(x_hbm.at[0:6], xv.at[0:6]), (wq_hbm.at[0], wq), (x_hbm.at[6:12], xv.at[6:12]), (wp_hbm.at[0], wp)], sem
    )
    small = Inputs(
        [
            (region_hbm, region_ref), (pick_hbm, pick_ref), (lane_hbm, lane_ref), (adds_hbm, adds_ref),
            (g1_hbm, g1_ref), (g2_hbm, g2_ref),
        ],
        small_sem,
    )
    first_row = (lax.axis_index("lat") == 0).astype(F32)
    small.wait(*range(6))
    g1, g2 = g1_ref[0:1, :], g2_ref[0:1, :]
    tiles, features, strides = [], [], []
    for half in range(2):
        lab1, lab2 = token_labels(region_ref, half, pick_ref, lane_ref, adds_ref, lab_s, first_row)
        features += [(query_features(lab1[p], 144), key_features(lab1[p], 144)) for p in (slice(0, 144), slice(144, 288))]
        for i in range(2):
            for side in range(2):
                start = (i * 2 + side) * GROUP
                labs[start : start + GROUP, :] = jnp.broadcast_to(grouped(lab2, i, side), (GROUP, 128))
        tiles.append(jnp.transpose(labs[...], (1, 0))[0:8])
    for half in range(2):
        inputs.wait(2 * half)
        for n in range(half * 72, half * 72 + 72):
            store_rows(xs, slice(n * LEV, (n + 1) * LEV), xv[n // COLS, n % COLS].astype(F32))
        strides += [pl.ds(half * HALF + level, PER_LEVEL, stride=LEV) for level in range(LEV)]
    x = jnp.concatenate([load_rows(xs, rows) for rows in strides], axis=0)
    a = layer_norm(x, g1).astype(BF)
    inputs.wait(1)
    mlp_inputs = Inputs(mlp_chunks(wu_hbm, wd_hbm, 0, wu, wd), mlp_sem)
    qkv = jnp.dot(a, wq[...], preferred_element_type=F32).astype(BF)
    parts = []
    for i, (qf, kf) in enumerate(features):
        p = slice(i * 144, (i + 1) * 144)
        parts.append((qkv[p, :D], qkv[p, D : 2 * D], qkv[p, 2 * D :], qf, kf))
    o = jnp.concatenate(attend_all(parts), axis=0).astype(BF)
    inputs.wait(3)
    h = x + jnp.dot(o, wp[...], preferred_element_type=F32)
    for i, rows in enumerate(strides):
        store_rows(xs, rows, h[i * PER_LEVEL : (i + 1) * PER_LEVEL])
    mid_ref[...] = load_rows(xs, slice(PER_RT, 3 * PER_RT))
    row = lax.broadcasted_iota(jnp.int32, (8, 384), 0)
    tile = jnp.where(row == 0, tiles[0], tiles[1])
    tile = jnp.concatenate([tile, jnp.zeros((8, 128), F32)], axis=1).astype(BF)
    tile_ref[...] = tile
    h = jnp.concatenate([load_rows(xs, slice(0, PER_RT)), load_rows(xs, slice(3 * PER_RT, TOKENS))], axis=0)
    y = mlp(h, g2, wu, wd, mlp_inputs.wait, FF)
    odd = is_odd("lat")
    for side in range(2):
        rows = slice(side * GROUP, (side + 1) * GROUP)
        up, down = grouped(y, 0, side), grouped(y, 1, side)
        one_ref[rows, :] = jnp.where(odd, up, down).astype(BF)
        two_ref[rows, :] = jnp.where(odd, down, up).astype(BF)
    one_ref[PER_RT:, :] = tile
    two_ref[PER_RT:, :] = tile


def middle_mlp_kernel(mid, tile_ref, g2_ref, wu, wd_hbm, wq_hbm, one_ref, two_ref, wq1, wd, sem):
    chunks = [slice(c, c + FCHUNK) for c in range(0, FF, FCHUNK)]
    inputs = Inputs([(wd_hbm.at[0, c], wd.at[c]) for c in chunks] + [(wq_hbm.at[1], wq1)], sem)
    y = mlp(mid[...], g2_ref[0:1, :], wu, wd, lambda up, down: inputs.wait(down // 2))
    odd = is_odd("lon")
    for i in range(2):
        rows = slice(i * GROUP, (i + 1) * GROUP)
        left, right = grouped(y, i, 0), grouped(y, i, 1)
        one_ref[rows, :] = jnp.where(odd, left, right).astype(BF)
        two_ref[rows, :] = jnp.where(odd, right, left).astype(BF)
    one_ref[PER_RT:, :] = tile_ref[...]
    two_ref[PER_RT:, :] = tile_ref[...]
    inputs.wait(N_CHUNK // 2)


class Either:
    def __init__(self, odd, first, second):
        self.odd, self.first, self.second = odd, first, second

    def __getitem__(self, at):
        return jnp.where(self.odd, self.first[at].astype(F32), self.second[at].astype(F32))


def both_ways(axis, one, two):
    odd = is_odd(axis)
    return Either(odd, one, two), Either(odd, two, one)


def pack_kernel(own_one, own_two, one, two, first_ref, second_ref):
    up, down = both_ways("lat", own_one, own_two)
    above, below = both_ways("lat", one, two)
    odd = is_odd("lon")
    for i, v in enumerate((up, down, above, below)):
        left, right = (v[side * GROUP : (side + 1) * GROUP, :] for side in range(2))
        rows = slice(i * GROUP, (i + 1) * GROUP)
        first_ref[rows, :] = jnp.where(odd, left, right).astype(BF)
        second_ref[rows, :] = jnp.where(odd, right, left).astype(BF)
    for i, v in enumerate((up, above, below)):
        rows = slice(4 * GROUP + 8 * i, 4 * GROUP + 8 * i + 8)
        tile = v[PER_RT:, :].astype(BF)
        first_ref[rows, :] = tile
        second_ref[rows, :] = tile


def columns_of(tile):
    t = jnp.transpose(tile.astype(F32)[:, :384], (1, 0))
    return [t[(g % 4) * GROUP : (g % 4 + 1) * GROUP, g // 4 : g // 4 + 1] for g in range(8)]


def second_body(arrays, windows_of, g1_ref, g2_ref, hbm, weights, out_hbm, scratch, rts):
    o_s, x_s, y_s, out_sem, *sem = scratch
    wq, wp, wu, wd = weights
    arrived = (lambda *which: None) if hbm is None else Inputs(second_copies(hbm, weights), sem[0]).wait
    g1, g2 = g1_ref[1:2, :], g2_ref[1:2, :]
    windows, parts, inner = windows_of(*arrays), [], []
    for own, halo in windows:
        n_own = len(own) * GROUP
        x = jnp.concatenate([s[0].astype(F32) for s in own + halo], axis=0)
        lab = jnp.concatenate([s[1] for s in own + halo], axis=0)
        a = layer_norm(x, g1).astype(BF)
        kv = jnp.dot(a, wq[:, D:], preferred_element_type=F32).astype(BF)
        q = jnp.dot(a[:n_own], wq[:, :D], preferred_element_type=F32).astype(BF)
        inner.append(x[:n_own])
        parts.append((q, kv[:, :D], kv[:, D:], query_features(lab[:n_own], n_own), key_features(lab, 4 * GROUP)))
    for (own, _), x, o in zip(windows, inner, attend_all(parts)):
        for i, s in enumerate(own):
            at, side = s[2]
            for r in range(3):
                rows = piece(at * 3 + r, side)
                o_s[rows, :] = o[i * GROUP + r * PIECE : i * GROUP + (r + 1) * PIECE]
                x_s[rows, :] = x[i * GROUP + r * PIECE : i * GROUP + (r + 1) * PIECE]
    arrived(0)
    h = x_s[...] + jnp.dot(o_s[...].astype(BF), wp[...], preferred_element_type=F32)
    o_s[...] = mlp(h, g2, wu, wd, lambda *which: arrived(*[1 + w for w in which]), FF if hbm is None else FCHUNK)
    copies = []
    for i, rt in enumerate(rts):
        for n in range(36):
            t = i * PER_RT + n * LEV
            y_s[i * 3 + n // COLS, n % COLS] = o_s[t : t + LEV, :].astype(BF)
        c = pltpu.make_async_copy(y_s.at[i * 3 : i * 3 + 3], out_hbm.at[rt * 3 : rt * 3 + 3], out_sem.at[i])
        c.start()
        copies.append(c)
    for c in copies:
        c.wait()


def rows_of(ref, i):
    return ref[i * GROUP : (i + 1) * GROUP, :]


def middle_windows(own_one, own_two, one, two):
    left, right = both_ways("lon", own_one, own_two)
    left_halo, right_halo = both_ways("lon", one, two)
    mine = columns_of(left[PER_RT:, :])
    windows = []
    for side, (own_ref, halo_ref) in enumerate(((left, left_halo), (right, right_halo))):
        theirs = columns_of(halo_ref[PER_RT:, :])
        own = [(rows_of(own_ref, rt - 1), mine[rt * 2 + side], (rt - 1, side)) for rt in (1, 2)]
        halo = [(rows_of(halo_ref, rt - 1), theirs[rt * 2 + 1 - side]) for rt in (1, 2)]
        windows.append((own, halo))
    return windows


def edge_windows(own_one, own_two, v_one, v_two, h_one, h_two):
    up, down = both_ways("lat", own_one, own_two)
    above, below = both_ways("lat", v_one, v_two)
    left_halo, right_halo = both_ways("lon", h_one, h_two)
    mine = columns_of(up[PER_RT:, :])
    beside = []
    for ref in (left_halo, right_halo):
        beside.append([columns_of(ref[4 * GROUP + 8 * i : 4 * GROUP + 8 * i + 8, :]) for i in range(3)])
    windows = []
    for at, (rt, own_ref, v_ref) in enumerate(((0, up, above), (3, down, below))):
        theirs = columns_of(v_ref[PER_RT:, :])
        for side, ref in enumerate((left_halo, right_halo)):
            labels = beside[side]
            own = [(rows_of(own_ref, side), mine[rt * 2 + side], (at, side))]
            halo = [
                (rows_of(v_ref, side), theirs[(3 - rt) * 2 + side]),
                (rows_of(ref, at), labels[0][rt * 2 + 1 - side]),
                (rows_of(ref, 2 + at), labels[1 + at][(3 - rt) * 2 + 1 - side]),
            ]
            windows.append((own, halo))
    return windows


def second_copies(hbm, weights):
    wp_hbm, wu_hbm, wd_hbm = hbm
    wp, wu, wd = weights[1:]
    return [(wp_hbm.at[1], wp)] + mlp_chunks(wu_hbm, wd_hbm, 1, wu, wd)


def middle_kernel(a, b, c, d, g1_ref, g2_ref, wq, wp_hbm, wu_hbm, wd_hbm, out_hbm, wp, wu, wd, *scratch):
    hbm = (wp_hbm, wu_hbm, wd_hbm)
    second_body((a, b, c, d), middle_windows, g1_ref, g2_ref, hbm, (wq, wp, wu, wd), out_hbm, scratch, (1, 2))


def edge_kernel(out_in, a, b, c, d, e, f, g1_ref, g2_ref, wq, wp, wu, wd, out_hbm, *scratch):
    weights = (wq, wp, wu, wd)
    second_body((a, b, c, d, e, f), edge_windows, g1_ref, g2_ref, None, weights, out_hbm, scratch, (0, 3))


WEIGHT_SCRATCH = [pltpu.VMEM((D, 3 * D), BF), pltpu.VMEM((D, D), BF)]


def dma(n):
    return pltpu.SemaphoreType.DMA((n,))


SECOND_SCRATCH = [
    pltpu.VMEM((HALF, D), F32),
    pltpu.VMEM((HALF, D), F32),
    pltpu.VMEM((6, COLS, LEV, D), BF),
    dma(2),
]

VM = pl.BlockSpec(memory_space=pltpu.VMEM)
ANY = pl.BlockSpec(memory_space=pl.ANY)
HBM = pl.BlockSpec(memory_space=pltpu.HBM)


def cost(flops, nbytes):
    return pl.CostEstimate(flops=int(flops), bytes_accessed=int(nbytes), transcendentals=0)


def in_hbm(value):
    return pltpu.with_memory_space_constraint(value, pltpu.HBM)


def exchange(one, two, axis):
    count = lax.axis_size(axis)
    even_pairs = [(s, s + 1 - 2 * (s % 2)) for s in range(count)]
    odd_pairs = [(s, (s - 1 + 2 * (s % 2)) % count) for s in range(count)]
    return lax.ppermute(one, axis, even_pairs), lax.ppermute(two, axis, odd_pairs)


def first_calls(tokens, region, g1, g2, weights):
    pick, lane, adds = token_tables()
    tables = [in_hbm(jnp.asarray(t, d)) for t, d in ((pick, BF), (lane, BF), (adds, F32))]
    params = pltpu.CompilerParams(vmem_limit_bytes=VMEM_LIMIT)
    edge_out = jax.ShapeDtypeStruct((PER_RT + 8, D), BF)
    up, down, tile, mid, wu, g1, g2 = pl.pallas_call(
        first_kernel,
        out_shape=(
            edge_out, edge_out, pltpu.VMEM((8, D), BF), pltpu.VMEM((HALF, D), F32),
            pltpu.VMEM((D, FF), BF), pltpu.VMEM((2, D), F32), pltpu.VMEM((2, D), F32),
        ),
        in_specs=[HBM] * 11,
        out_specs=[VM] * 7,
        scratch_shapes=[
            pltpu.VMEM((ROWS, COLS, LEV, D), BF), pltpu.VMEM((D // 128, TOKENS, 128), F32), pltpu.VMEM((HALF, 128), F32),
            pltpu.VMEM((384, 128), F32), pltpu.VMEM((ROWS, LEV, COLS), jnp.int32), pltpu.VMEM((HALF, 128), BF),
            pltpu.VMEM((HALF, 128), BF), pltpu.VMEM((HALF, 128), F32),
        ] + WEIGHT_SCRATCH + [pltpu.VMEM((FF, D), BF), dma(4), dma(N_CHUNK), dma(6)],
        compiler_params=params,
        cost_estimate=cost(4e9, 8e6),
        name="first_block",
    )(tokens, region, *tables, g1, g2, *weights)
    left, right, early = pl.pallas_call(
        middle_mlp_kernel,
        out_shape=(edge_out, edge_out, pltpu.VMEM((D, 3 * D), BF)),
        in_specs=[VM] * 4 + [HBM] * 2,
        out_specs=[VM] * 3,
        scratch_shapes=[pltpu.VMEM((FF, D), BF), dma(N_CHUNK // 2 + 1)],
        compiler_params=params,
        cost_estimate=cost(1.3e9, 5e6),
        name="first_middle",
    )(mid, tile, g2, wu, weights[3], weights[0])
    return up, down, left, right, g1, g2, early


def second_calls(middle, edge, g1, g2, early, weights):
    params = pltpu.CompilerParams(vmem_limit_bytes=VMEM_LIMIT)
    out_shape = jax.ShapeDtypeStruct((ROWS, COLS, LEV, D), BF)
    out, *late = pl.pallas_call(
        middle_kernel,
        out_shape=(
            out_shape, pltpu.VMEM((D, D), BF), pltpu.VMEM((D, FF), BF), pltpu.VMEM((FF, D), BF),
        ),
        in_specs=[VM] * 7 + [HBM] * 3,
        out_specs=[HBM] + [VM] * 3,
        scratch_shapes=SECOND_SCRATCH + [dma(1 + N_CHUNK)],
        compiler_params=params,
        cost_estimate=cost(2.5e9, 8e6),
        name="second_middle",
    )(*middle, g1, g2, early, *weights[1:])
    return pl.pallas_call(
        edge_kernel,
        out_shape=out_shape,
        in_specs=[HBM] + [VM] * 12,
        out_specs=HBM,
        scratch_shapes=SECOND_SCRATCH,
        input_output_aliases={0: 0},
        compiler_params=params,
        cost_estimate=cost(2.5e9, 8e6),
        name="second_edge",
    )(out, *edge, g1, g2, early, *late)


def per_device(tokens, region, norm_gain1, qkv_weight, proj_weight, norm_gain2, up_weight, down_weight):
    weights = [in_hbm(w) for w in (qkv_weight, proj_weight, up_weight, down_weight)]
    g1, g2 = in_hbm(norm_gain1), in_hbm(norm_gain2)
    up, down, left, right, g1, g2, early = first_calls(
        in_hbm(jnp.transpose(tokens, (1, 2, 0, 3))), in_hbm(jnp.transpose(region, (1, 0, 2))), g1, g2, weights
    )
    received = exchange(up, down, "lat")
    above, below = received
    left, right, above = lax.optimization_barrier((left, right, above))
    halo = exchange(left, right, "lon")
    message = jax.ShapeDtypeStruct((4 * GROUP + 24, D), BF)
    packed = pl.pallas_call(
        pack_kernel,
        out_shape=(message, message),
        in_specs=[VM] * 4,
        out_specs=[VM] * 2,
        compiler_params=pltpu.CompilerParams(vmem_limit_bytes=8 * 1024 * 1024),
        cost_estimate=cost(1e6, 1e6),
        name="pack_edges",
    )(up, down, above, below)
    beside = exchange(*packed, "lon")
    out = second_calls((left, right, *halo), (up, down, above, below, *beside), g1, g2, early, weights)
    return jnp.transpose(out, (2, 0, 1, 3))


def solution(mesh):
    return jax.shard_map(
        per_device,
        mesh=mesh,
        in_specs=(P(None, "lat", "lon", None), P(None, "lat", "lon"), P(), P(), P(), P(), P(), P()),
        out_specs=P(None, "lat", "lon", None),
        check_vma=False,
    )
```
